256 devices in a mesh: row: 16 (over z_hi, x), col: 16 (over y, z_lo, core).
Axes of the slice: x: 4, y: 4, z: 8 (z_hi: 4, z_lo: 2; z = z_hi * 2 + z_lo), core: 2. Of those that a mesh axis runs over, the one named last changes fastest.
Arguments:
- start_vectors: float32 [64, 32768], P(None, ('row', 'col')), may hold values from -6 to 6
- scaling: float32 [32768], P(('row', 'col')), may hold values from 0.25 to 1.75
- block_values: bfloat16 [16, 16, 128, 128, 128], P('row', 'col'), may hold values from -0.046875 to 0.046875
- block_places: int32 [16, 16, 2, 128], P('row', 'col'), may hold values from 0 to 15, as said below
- block_counts: int32 [16, 16], P('row', 'col'), may hold values from 16 to 128, as said below
Outputs:
- filtered: float32 [64, 32768], P(None, ('row', 'col'))
The draws below stay inside these ranges and needn't reach their ends.
Inputs may be any that keep to these rules, and one draw needn't show every extreme that they name: `block_places`: within each device's 128 slots the positions (block row, block column) are distinct; entry 0 is the local block row (below 16), entry 1 the local block column (below 16). Slots at or after the device's count are not part of the matrix. `block_counts`: some device has all 128 slots live.
All inputs are finite; a program needn't handle non-finite values.
Results may differ from the reference program's by a relative error of at most 0.0038.
Values may be sent and summed in bfloat16 or wider, within the bound.
A program may use at most 128 MiB of HBM per device.

```python
import jax
import jax.numpy as jnp
from jax import lax

BLOCK = 128
VEC = 64
CAP = 128
STEPS = 3
GRID_R = 16
GRID_C = 16
TB = 16
TBC = 16
ORDER = 32768


def draw_block_places(key, part):
    device_keys = jax.random.split(jax.random.fold_in(key, 11), GRID_R * GRID_C)

    def one_device(device_key):
        slot_order = jax.random.permutation(device_key, TB * TBC)[:CAP].astype(jnp.int32)
        return jnp.stack([slot_order // TBC, slot_order % TBC])
    return jax.vmap(one_device)(device_keys).reshape(GRID_R, GRID_C, 2, CAP).astype(jnp.int32)


def draw_block_counts(key, part):
    base_key = jax.random.fold_in(key, 23)
    key_base, key_heavy, key_forced = jax.random.split(base_key, 3)
    devices_n = GRID_R * GRID_C
    base_counts = jax.random.randint(key_base, (devices_n,), CAP // 8, CAP // 2 + 1)
    heavy_mask = jax.random.randint(key_heavy, (devices_n,), 0, 8) == 0
    forced = jax.random.randint(key_forced, (), 0, devices_n)
    is_full = heavy_mask | (jnp.arange(devices_n) == forced)
    counts = jnp.where(is_full, CAP, base_counts)
    return counts.reshape(GRID_R, GRID_C).astype(jnp.int32)


def block_levels(stream_key, dims, pieces, least, largest):
    gain = 1.0
    for axis_at, shards_of in pieces:
        heights = jax.random.uniform(jax.random.fold_in(jax.random.fold_in(stream_key, 6), axis_at), (shards_of,), jnp.float32, least / len(pieces), largest / len(pieces))
        gain = gain * jnp.repeat(jnp.exp(heights), dims[axis_at] // shards_of).reshape((-1,) + (1,) * (len(dims) - 1 - axis_at))
    return gain


def scatter_about(rng, extent, spread, limit, cuts=(), held_as=jnp.bfloat16):
    gain = block_levels(rng, extent, cuts, -0.22, 0.18) if cuts else 1.0
    drawn = jax.random.normal(rng, extent, jnp.float32) * spread * gain
    return jnp.minimum(jnp.maximum(drawn, -limit), limit).astype(held_as)


def setup_inputs(seed: int = 0) -> dict:
    arg_keys = jax.random.split(jax.random.key(seed), 6)
    start_vectors = scatter_about(arg_keys[0], (VEC, ORDER), 1.0, 6.0, ((1, 256),), jnp.float32)
    scaling = jnp.clip(1.0 + 0.15 * jax.random.normal(arg_keys[1], (ORDER,), jnp.float32), 0.25, 1.75)
    block_values = scatter_about(arg_keys[2], (GRID_R, GRID_C, CAP, BLOCK, BLOCK), (CAP * BLOCK) ** -0.5, 0.046875, ((0, 16), (1, 16)))
    block_places = draw_block_places(jax.random.fold_in(arg_keys[5], 71), 0)
    block_counts = draw_block_counts(jax.random.fold_in(arg_keys[5], 71), 0)
    return {"start_vectors": start_vectors, "scaling": scaling, "block_values": block_values, "block_places": block_places, "block_counts": block_counts}


center_shift = 0.5
half_width = 3.0


def apply_matrix(scaled, block_values, block_places, block_counts):
    block_total = ORDER // BLOCK
    blocked = scaled.astype(jnp.float32).reshape(VEC, block_total, BLOCK)

    def one_device(totals, device_flat):
        grid_row = device_flat // GRID_C
        grid_col = device_flat % GRID_C
        slabs = block_values[grid_row, grid_col].astype(jnp.float32)
        places = block_places[grid_row, grid_col]
        glob_rows = (grid_row * TB + places[0]).astype(jnp.int32)
        glob_cols = (grid_col * TBC + places[1]).astype(jnp.int32)
        live_mask = (jnp.arange(CAP) < block_counts[grid_row, grid_col]).astype(jnp.float32)
        col_vecs = blocked[:, glob_cols, :]
        row_vecs = blocked[:, glob_rows, :]
        direct = jnp.einsum('gik,ngk->ngi', slabs, col_vecs) * live_mask[None, :, None]
        transposed = jnp.einsum('gik,ngi->ngk', slabs, row_vecs) * live_mask[None, :, None]
        totals = totals.at[:, glob_rows, :].add(direct)
        totals = totals.at[:, glob_cols, :].add(transposed)
        return totals, None

    zeros = jnp.zeros((VEC, block_total, BLOCK), jnp.float32)
    totals, _ = lax.scan(one_device, zeros, jnp.arange(GRID_R * GRID_C).astype(jnp.int32))
    return totals.reshape(VEC, ORDER)


def reference(start_vectors, scaling, block_values, block_places, block_counts):
    current = start_vectors
    previous = start_vectors
    for iterate in range(STEPS):
        scaled = (scaling[None, :] * current).astype(jnp.bfloat16)
        applied = apply_matrix(scaled, block_values, block_places, block_counts)
        mapped = scaling[None, :] * applied - center_shift * current
        if iterate == 0:
            updated = mapped / half_width
        else:
            updated = (2.0 / half_width) * mapped - previous
        previous = current
        current = updated
    return current
```

```python
import functools

import jax
import jax.numpy as jnp
from jax import lax
from jax.experimental import pallas as pl
from jax.experimental.pallas import tpu as pltpu
from jax.sharding import PartitionSpec as P

STEPS = 3
G = 16
B = 128
V = 64
S = 128
MESH = pl.DeviceIdType.MESH

center_shift = 0.5
half_width = 3.0


def kernel(table, x_ref, scale_ref, blocks_hbm, out_ref, blk, tile, cur, prev, piece, vrow, vcol, dsend, tsend, drecv, trecv,
           blk_sem, send_sem, recv_sem):
    r = lax.axis_index("row")
    c = lax.axis_index("col")
    diag = r == c

    load = pltpu.make_async_copy(blocks_hbm, blk.at[pl.ds(0, S)], blk_sem)
    load.start()

    barrier = pltpu.get_barrier_semaphore()

    def signal(row, col):
        pl.semaphore_signal(barrier, inc=1, device_id=(row, col), device_id_type=MESH)

    def greet(k, _):
        signal(lax.rem(r + k, G), r)
        signal(r, lax.rem(c + k, G))
        return 0

    lax.fori_loop(1, G, greet, 0)

    @pl.when(jnp.logical_not(diag))
    def _():
        def greet_col(k, _):
            signal(c, lax.rem(r + k, G))
            return 0

        lax.fori_loop(1, G, greet_col, 0)

    cur[...] = x_ref[...]
    prev[...] = jnp.zeros((V, B), jnp.float32)
    blk[S] = jnp.zeros((B, B), jnp.bfloat16)
    load.wait()

    def build(i, _):
        for j in range(G):
            tile[pl.ds(pl.multiple_of(i * B, B), B), pl.ds(j * B, B)] = blk[table[i * G + j]]
        return 0

    lax.fori_loop(0, G, build, 0)

    pl.semaphore_wait(barrier, jnp.where(diag, 2, 3) * (G - 1))

    def post(src, dst, kind, step, row, col):
        own = jnp.logical_and(row == r, col == c)

        @pl.when(own)
        def _():
            pltpu.make_async_copy(src, dst, recv_sem.at[kind, step]).start()

        @pl.when(jnp.logical_not(own))
        def _():
            pltpu.make_async_remote_copy(src, dst, send_sem.at[kind, step], recv_sem.at[kind, step], device_id=(row, col),
                                         device_id_type=MESH).start()

    def arrive(buf, kind, step):
        pltpu.make_async_copy(buf.at[step], buf.at[step], recv_sem.at[kind, step]).wait()

    def one_step(step, _):
        scale = scale_ref[...]
        piece[step] = (scale * cur[...]).astype(jnp.bfloat16)

        def share_cols(k, _):
            post(piece.at[step], vcol.at[step, c], 1, step, lax.rem(r + k, G), r)
            return 0

        def share_rows(k, _):
            post(piece.at[step], vrow.at[step, c], 0, step, r, lax.rem(c + k, G))
            return 0

        lax.fori_loop(0, G, share_rows, 0)
        lax.fori_loop(0, G, share_cols, 0)

        arrive(vrow, 0, step)

        def transposed(n, _):
            acc = jnp.zeros((V, 2 * B), jnp.float32)
            for k in range(G // 2):
                v = jnp.concatenate([vrow[step, 2 * k], vrow[step, 2 * k + 1]], axis=1)
                w = tile[pl.ds(2 * k * B, 2 * B), pl.ds(pl.multiple_of(n * 2 * B, 2 * B), 2 * B)]
                acc += jnp.dot(v, w, preferred_element_type=jnp.float32)
            for u in range(2):
                j = 2 * n + u
                tsend[step, j] = acc[:, u * B : (u + 1) * B].astype(jnp.bfloat16)
                post(tsend.at[step, j], trecv.at[step, r], 2, step, c, j)
            return 0

        lax.fori_loop(0, G // 2, transposed, 0)

        arrive(vcol, 1, step)

        def direct(n, _):
            acc = jnp.zeros((V, 2 * B), jnp.float32)
            for k in range(G // 2):
                v = jnp.concatenate([vcol[step, 2 * k], vcol[step, 2 * k + 1]], axis=1)
                w = tile[pl.ds(pl.multiple_of(n * 2 * B, 2 * B), 2 * B), pl.ds(2 * k * B, 2 * B)]
                acc += lax.dot_general(v, w, (((1,), (1,)), ((), ())), preferred_element_type=jnp.float32)
            for u in range(2):
                j = 2 * n + u
                dsend[step, j] = acc[:, u * B : (u + 1) * B].astype(jnp.bfloat16)
                post(dsend.at[step, j], drecv.at[step, c], 3, step, r, j)
            return 0

        lax.fori_loop(0, G // 2, direct, 0)

        arrive(trecv, 2, step)
        arrive(drecv, 3, step)
        applied = jnp.zeros((V, B), jnp.float32)
        for k in range(G):
            applied += trecv[step, k].astype(jnp.float32)
            applied += drecv[step, k].astype(jnp.float32)
        now = cur[...]
        mapped = scale * applied - center_shift * now
        first = step == 0
        factor = jnp.where(first, 1.0 / half_width, 2.0 / half_width)
        updated = factor * mapped - prev[...]
        prev[...] = now
        cur[...] = updated
        return 0

    lax.fori_loop(0, STEPS, one_step, 0)
    out_ref[...] = cur[...]

    def drain(step, _):
        for kind, buf in enumerate((vrow, vcol, tsend, dsend)):
            sent = buf.at[step, pl.ds(0, G - 1)]
            pltpu.make_async_copy(sent, sent, send_sem.at[kind, step]).wait()

        @pl.when(jnp.logical_not(diag))
        def _():
            for kind, buf in ((1, vcol), (2, tsend)):
                sent = buf.at[step, pl.ds(0, 1)]
                pltpu.make_async_copy(sent, sent, send_sem.at[kind, step]).wait()

        return 0

    lax.fori_loop(0, STEPS, drain, 0)


def per_device(start_vectors, scaling, block_values, block_places, block_counts):
    blocks = block_values.reshape(S, B, B)
    places = block_places.reshape(2, S)
    slots = jnp.arange(S, dtype=jnp.int32)
    at = jnp.where(slots < block_counts.reshape(()), places[0] * G + places[1], -1)
    hit = at[None, :] == jnp.arange(G * G, dtype=jnp.int32)[:, None]
    table = jnp.min(jnp.where(hit, slots[None, :], S), axis=1)
    vmem = pl.BlockSpec(memory_space=pltpu.VMEM)
    slab = pltpu.VMEM((STEPS, G, V, B), jnp.bfloat16)
    return pl.pallas_call(
        kernel,
        name="filter",
        out_shape=jax.ShapeDtypeStruct((V, B), jnp.float32),
        in_specs=[pl.BlockSpec(memory_space=pltpu.SMEM), vmem, vmem, pl.BlockSpec(memory_space=pl.ANY)],
        out_specs=vmem,
        scratch_shapes=[
            pltpu.VMEM((S + 1, B, B), jnp.bfloat16),
            pltpu.VMEM((G * B, G * B), jnp.bfloat16),
            pltpu.VMEM((V, B), jnp.float32),
            pltpu.VMEM((V, B), jnp.float32),
            pltpu.VMEM((STEPS, V, B), jnp.bfloat16),
            slab, slab, slab, slab, slab, slab,
            pltpu.SemaphoreType.DMA,
            pltpu.SemaphoreType.DMA((4, STEPS)),
            pltpu.SemaphoreType.DMA((4, STEPS)),
        ],
        compiler_params=pltpu.CompilerParams(collective_id=0, has_side_effects=True, vmem_limit_bytes=48 << 20),
    )(table, start_vectors, scaling.reshape(1, B), blocks)


def solution(mesh):
    in_specs = (
        P(None, ("row", "col")),
        P(("row", "col")),
        P("row", "col", None, None, None),
        P("row", "col", None, None),
        P("row", "col"),
    )
    out_specs = P(None, ("row", "col"))
    return jax.shard_map(
        per_device, mesh=mesh, in_specs=in_specs, out_specs=out_specs, check_vma=False
    )
```

```python
import jax
import jax.numpy as jnp
from jax import lax
from jax.experimental import pallas as pl
from jax.experimental.pallas import tpu as pltpu
from jax.sharding import PartitionSpec as P

STEPS = 3
G = 16
Q = 4
B = 128
V = 64
S = 128
MESH = pl.DeviceIdType.MESH
VROW, HOP, VCOL, PART, SUMS, DIRECT = range(6)

center_shift = 0.5
half_width = 3.0


def kernel(x_hbm, scale_hbm, places_hbm, count_hbm, blocks_hbm, out_ref, blk, tile, cur, prev, scale_ref, places, count,
           table_v, table, piece, hop, vrow, vcol, tsend, dsend, part, sums_send, sums, drecv, in_sem, send_sem, recv_sem,
           hop_sem):
    r = lax.axis_index("row")
    c = lax.axis_index("col")
    r_hi, r_lo = r // Q, lax.rem(r, Q)
    c_hi, c_lo = c // Q, lax.rem(c, Q)
    home = r_lo == c_lo

    loads = [
        pltpu.make_async_copy(src, dst, in_sem.at[i])
        for i, (src, dst) in enumerate(((x_hbm, cur), (scale_hbm, scale_ref), (places_hbm, places), (count_hbm, count),
                                        (blocks_hbm, blk.at[pl.ds(0, S)])))
    ]
    for load in loads:
        load.start()

    barrier = pltpu.get_barrier_semaphore()

    def signal(row, col):
        pl.semaphore_signal(barrier, inc=1, device_id=(row, col), device_id_type=MESH)

    def greet_row(k, _):
        signal(r, lax.rem(c + k, G))
        return 0

    lax.fori_loop(1, G, greet_row, 0)
    for k in range(1, Q):
        signal(lax.rem(r + Q * k, G), c)

    def greet_plane(k, _):
        row = r_hi * Q + lax.rem(r_lo + 1 + k // Q, Q)
        signal(row, lax.rem(k, Q) * Q + r_lo)
        return 0

    lax.fori_loop(0, Q * (Q - 1), greet_plane, 0)

    @pl.when(jnp.logical_not(home))
    def _():
        def greet_other(k, _):
            lo = lax.rem(r_lo + 1 + lax.rem(k, Q - 1), Q)
            signal(r_hi * Q + c_lo, (k // (Q - 1)) * Q + lo)
            return 0

        lax.fori_loop(0, Q * (Q - 1), greet_other, 0)

    prev[...] = jnp.zeros((V, B), jnp.float32)
    blk[S] = jnp.zeros((B, B), jnp.bfloat16)

    loads[2].wait()
    loads[3].wait()
    lane = lax.broadcasted_iota(jnp.int32, (1, S), 1)
    at = jnp.where(lane < count[...], places[0:1, :] * G + places[1:2, :], -1)
    row_id = lax.broadcasted_iota(jnp.int32, (S, S), 0)
    col_id = lax.broadcasted_iota(jnp.int32, (S, S), 1)
    for half in range(2):
        slot = jnp.min(jnp.where(row_id + half * S == at, col_id, S), axis=1, keepdims=True)
        table_v[half : half + 1, :] = jnp.min(jnp.where(row_id == col_id, slot, S), axis=0, keepdims=True)
    to_scalars = pltpu.make_async_copy(table_v, table, in_sem.at[5])
    to_scalars.start()
    loads[0].wait()
    loads[1].wait()

    pl.semaphore_wait(barrier, jnp.where(home, 15 + 3 + 12, 15 + 3 + 12 + 12))

    def post(src, dst, kind, step, row, col):
        own = jnp.logical_and(row == r, col == c)

        @pl.when(own)
        def _():
            pltpu.make_async_copy(src, dst, recv_sem.at[kind, step]).start()

        @pl.when(jnp.logical_not(own))
        def _():
            pltpu.make_async_remote_copy(src, dst, send_sem.at[kind, step], recv_sem.at[kind, step], device_id=(row, col),
                                         device_id_type=MESH).start()

    def arrive(buf, kind, step):
        pltpu.make_async_copy(buf.at[step], buf.at[step], recv_sem.at[kind, step]).wait()

    def share(step):
        piece[step] = (scale_ref[...] * cur[...]).astype(jnp.bfloat16)

        def along_row(k, _):
            post(piece.at[step], vrow.at[step, c], VROW, step, r, lax.rem(c + k, G))
            return 0

        def hop_to(k):
            return pltpu.make_async_remote_copy(piece.at[step], hop.at[step, k - 1], send_sem.at[HOP, step],
                                                hop_sem.at[step, k - 1], device_id=(lax.rem(r + Q * k, G), c),
                                                device_id_type=MESH)

        def spread(src, k):
            col = lax.rem(r_hi + Q - k, Q) * Q + r_lo

            def to(i, _):
                post(src, vcol.at[step, c], VCOL, step, r_hi * Q + lax.rem(r_lo + i, Q), col)
                return 0

            lax.fori_loop(0, Q, to, 0)

        hops = [hop_to(k) for k in (2, 1, 3)]
        for h in hops:
            h.start()
        lax.fori_loop(0, G, along_row, 0)
        spread(piece.at[step], 0)
        for k in (1, 3, 2):
            pltpu.make_async_copy(hop.at[step, k - 1], hop.at[step, k - 1], hop_sem.at[step, k - 1]).wait()
            spread(hop.at[step, k - 1], k)

    def multiply(step):
        with jax.named_scope("wait_vrow"):
            arrive(vrow, VROW, step)

        def transposed(n, _):
            acc = jnp.zeros((V, 2 * B), jnp.float32)
            for k in range(G // 2):
                v = jnp.concatenate([vrow[step, 2 * k], vrow[step, 2 * k + 1]], axis=1)
                w = tile[pl.ds(2 * k * B, 2 * B), pl.ds(pl.multiple_of(n * 2 * B, 2 * B), 2 * B)]
                acc += jnp.dot(v, w, preferred_element_type=jnp.float32)
            for u in range(2):
                j = 2 * n + u
                tsend[step, j] = acc[:, u * B : (u + 1) * B].astype(jnp.bfloat16)
                post(tsend.at[step, j], part.at[step, r_lo * Q + c_hi], PART, step, r_hi * Q + c_lo, j)
            return 0

        with jax.named_scope("mm_transposed"):
            lax.fori_loop(0, G // 2, transposed, 0)

        with jax.named_scope("wait_vcol"):
            arrive(vcol, VCOL, step)

        def direct(n, _):
            acc = jnp.zeros((V, 2 * B), jnp.float32)
            for k in range(G // 2):
                v = jnp.concatenate([vcol[step, 2 * k], vcol[step, 2 * k + 1]], axis=1)
                w = tile[pl.ds(pl.multiple_of(n * 2 * B, 2 * B), 2 * B), pl.ds(2 * k * B, 2 * B)]
                acc += lax.dot_general(v, w, (((1,), (1,)), ((), ())), preferred_element_type=jnp.float32)
            for u in range(2):
                j = 2 * n + u
                dsend[step, j] = acc[:, u * B : (u + 1) * B].astype(jnp.bfloat16)
                post(dsend.at[step, j], drecv.at[step, c], DIRECT, step, r, j)
            return 0

        with jax.named_scope("mm_direct"):
            lax.fori_loop(0, G // 2, direct, 0)

    def collect(step):
        with jax.named_scope("wait_part"):
            arrive(part, PART, step)
        for k in (2, 1, 3, 0):
            hi = lax.rem(r_hi + k, Q)
            total = jnp.zeros((V, B), jnp.float32)
            for lo in range(Q):
                total += part[step, lo * Q + hi].astype(jnp.float32)
            if k == 0:
                applied = total
            else:
                sums_send[step, k - 1] = total.astype(jnp.bfloat16)
                pltpu.make_async_remote_copy(sums_send.at[step, k - 1], sums.at[step, k - 1], send_sem.at[SUMS, step],
                                             recv_sem.at[SUMS, step], device_id=(hi * Q + r_lo, c),
                                             device_id_type=MESH).start()
        with jax.named_scope("wait_drecv"):
            arrive(drecv, DIRECT, step)
        for k in range(G):
            applied += drecv[step, k].astype(jnp.float32)
        with jax.named_scope("wait_sums"):
            arrive(sums, SUMS, step)
        for k in range(Q - 1):
            applied += sums[step, k].astype(jnp.float32)
        now = cur[...]
        mapped = scale_ref[...] * applied - center_shift * now
        factor = jnp.where(step == 0, 1.0 / half_width, 2.0 / half_width)
        updated = factor * mapped - prev[...]
        prev[...] = now
        cur[...] = updated

    def one_step(step, _):
        with jax.named_scope("share"):
            share(step)

        @pl.when(step == 0)
        def _():
            with jax.named_scope("build"):
                to_scalars.wait()
                loads[4].wait()

                def build(i, _):
                    for j in range(G):
                        slot = jnp.clip(table[i // 8, lax.rem(i, 8) * G + j], 0, S)
                        tile[pl.ds(pl.multiple_of(i * B, B), B), pl.ds(j * B, B)] = blk[slot]
                    return 0

                lax.fori_loop(0, G, build, 0)

        multiply(step)
        collect(step)
        return 0

    lax.fori_loop(0, STEPS, one_step, 0)
    out_ref[...] = cur[...]

    def drain(step, _):
        for kind, buf, n in ((VROW, vrow, G - 1), (HOP, hop, Q - 1), (VCOL, vcol, G - 1), (PART, part, G - 1),
                             (SUMS, sums, Q - 1), (DIRECT, drecv, G - 1)):
            sent = buf.at[step, pl.ds(0, n)]
            pltpu.make_async_copy(sent, sent, send_sem.at[kind, step]).wait()

        @pl.when(jnp.logical_not(home))
        def _():
            for kind, buf in ((VCOL, vcol), (PART, part)):
                sent = buf.at[step, pl.ds(0, 1)]
                pltpu.make_async_copy(sent, sent, send_sem.at[kind, step]).wait()

        return 0

    with jax.named_scope("drain"):
        lax.fori_loop(0, STEPS, drain, 0)


def per_device(start_vectors, scaling, block_values, block_places, block_counts):
    anywhere = pl.BlockSpec(memory_space=pl.ANY)

    def slab(n):
        return pltpu.VMEM((STEPS, n, V, B), jnp.bfloat16)

    f32 = pltpu.VMEM((V, B), jnp.float32)
    return pl.pallas_call(
        kernel,
        name="filter",
        out_shape=jax.ShapeDtypeStruct((V, B), jnp.float32),
        in_specs=[anywhere] * 5,
        out_specs=pl.BlockSpec(memory_space=pltpu.VMEM),
        scratch_shapes=[
            pltpu.VMEM((S + 1, B, B), jnp.bfloat16),
            pltpu.VMEM((G * B, G * B), jnp.bfloat16),
            f32,
            f32,
            pltpu.VMEM((1, B), jnp.float32),
            pltpu.VMEM((2, S), jnp.int32),
            pltpu.VMEM((1, 1), jnp.int32),
            pltpu.VMEM((2, S), jnp.int32),
            pltpu.SMEM((2, S), jnp.int32),
            pltpu.VMEM((STEPS, V, B), jnp.bfloat16),
            slab(Q - 1), slab(G), slab(G), slab(G), slab(G), slab(G), slab(Q - 1), slab(Q - 1), slab(G),
            pltpu.SemaphoreType.DMA((6,)),
            pltpu.SemaphoreType.DMA((6, STEPS)),
            pltpu.SemaphoreType.DMA((6, STEPS)),
            pltpu.SemaphoreType.DMA((STEPS, Q - 1)),
        ],
        compiler_params=pltpu.CompilerParams(collective_id=0, has_side_effects=True, vmem_limit_bytes=60 << 20),
    )(start_vectors, scaling.reshape(1, B), block_places.reshape(2, S), block_counts, block_values.reshape(S, B, B))


def solution(mesh):
    in_specs = (
        P(None, ("row", "col")),
        P(("row", "col")),
        P("row", "col", None, None, None),
        P("row", "col", None, None),
        P("row", "col"),
    )
    out_specs = P(None, ("row", "col"))
    return jax.shard_map(
        per_device, mesh=mesh, in_specs=in_specs, out_specs=out_specs, check_vma=False
    )
```

```python
import jax
import jax.numpy as jnp
from jax import lax
from jax.experimental import pallas as pl
from jax.experimental.pallas import tpu as pltpu
from jax.sharding import PartitionSpec as P

STEPS = 3
G = 16
Q = 4
B = 128
V = 64
S = 128
MESH = pl.DeviceIdType.MESH
VROW, HOP, VCOL, PART, SUMS, DIRECT = range(6)

center_shift = 0.5
half_width = 3.0


def kernel(x_hbm, scale_hbm, places_hbm, count_hbm, blocks_hbm, out_ref, blk, tile, cur, prev, scale_ref, places, count,
           table_v, table, piece, hop, vrow, vcol, tsend, dsend, part, sums_send, sums, drecv, in_sem, send_sem, recv_sem,
           hop_sem):
    r = lax.axis_index("row")
    c = lax.axis_index("col")
    r_hi, r_lo = r // Q, lax.rem(r, Q)
    c_hi, c_lo = c // Q, lax.rem(c, Q)
    home_hi, home_lo = r_hi == c_hi, r_lo == c_lo

    loads = [
        pltpu.make_async_copy(src, dst, in_sem.at[i])
        for i, (src, dst) in enumerate(((x_hbm, cur), (scale_hbm, scale_ref), (places_hbm, places), (count_hbm, count),
                                        (blocks_hbm, blk.at[pl.ds(0, S)])))
    ]
    for load in loads:
        load.start()

    barrier = pltpu.get_barrier_semaphore()

    def signal(row, col):
        pl.semaphore_signal(barrier, inc=1, device_id=(row, col), device_id_type=MESH)

    for k in range(1, Q):
        signal(lax.rem(r_hi + k, Q) * Q + r_lo, r_hi * Q + c_lo)
        signal(r_hi * Q + lax.rem(r_lo + k, Q), c_hi * Q + r_lo)

    @pl.when(jnp.logical_not(home_hi))
    def _():
        for k in range(1, Q):
            signal(c_hi * Q + r_lo, lax.rem(r_hi + k, Q) * Q + c_lo)

    @pl.when(jnp.logical_not(home_lo))
    def _():
        for k in range(1, Q):
            signal(r_hi * Q + c_lo, c_hi * Q + lax.rem(r_lo + k, Q))

    def greet_row(k, _):
        signal(r, lax.rem(c + k, G))
        return 0

    lax.fori_loop(1, G, greet_row, 0)

    prev[...] = jnp.zeros((V, B), jnp.float32)
    blk[S] = jnp.zeros((B, B), jnp.bfloat16)

    loads[2].wait()
    loads[3].wait()
    lane = lax.broadcasted_iota(jnp.int32, (1, S), 1)
    at = jnp.where(lane < count[...], places[0:1, :] * G + places[1:2, :], -1)
    row_id = lax.broadcasted_iota(jnp.int32, (S, S), 0)
    col_id = lax.broadcasted_iota(jnp.int32, (S, S), 1)
    for half in range(2):
        slot = jnp.min(jnp.where(row_id + half * S == at, col_id, S), axis=1, keepdims=True)
        table_v[half : half + 1, :] = jnp.min(jnp.where(row_id == col_id, slot, S), axis=0, keepdims=True)
    to_scalars = pltpu.make_async_copy(table_v, table, in_sem.at[5])
    to_scalars.start()
    loads[0].wait()
    loads[1].wait()
    with jax.named_scope("load"):
        loads[4].wait()
        to_scalars.wait()

    def build(i, _):
        for j in range(G):
            slot = jnp.clip(table[i // 8, lax.rem(i, 8) * G + j], 0, S)
            tile[pl.ds(pl.multiple_of(i * B, B), B), pl.ds(j * B, B)] = blk[slot]
        return 0

    with jax.named_scope("build"):
        lax.fori_loop(0, G, build, 0)

    with jax.named_scope("barrier"):
        pl.semaphore_wait(barrier, G - 1 + jnp.where(home_hi, 3, 6) + jnp.where(home_lo, 3, 6))

    def post(src, dst, kind, step, row, col, arrival=None):
        own = jnp.logical_and(row == r, col == c)
        arrival = recv_sem.at[kind, step] if arrival is None else arrival

        @pl.when(own)
        def _():
            pltpu.make_async_copy(src, dst, arrival).start()

        @pl.when(jnp.logical_not(own))
        def _():
            pltpu.make_async_remote_copy(src, dst, send_sem.at[kind, step], arrival, device_id=(row, col),
                                         device_id_type=MESH).start()

    def arrive(buf, kind, step):
        pltpu.make_async_copy(buf.at[step], buf.at[step], recv_sem.at[kind, step]).wait()

    def share(step):
        piece[step] = (scale_ref[...] * cur[...]).astype(jnp.bfloat16)

        def along_row(k, _):
            post(piece.at[step], vrow.at[step, c], VROW, step, r, lax.rem(c + k, G))
            return 0

        for k in (2, 1, 3, 0):
            row, col = lax.rem(r_hi + k, Q) * Q + r_lo, r_hi * Q + c_lo
            post(piece.at[step], hop.at[step, c_hi], HOP, step, row, col, hop_sem.at[step, c_hi])
        lax.fori_loop(0, G, along_row, 0)
        for k in (0, 1, 3, 2):
            hi = lax.rem(c_hi + k, Q)
            pltpu.make_async_copy(hop.at[step, hi], hop.at[step, hi], hop_sem.at[step, hi]).wait()

            def spread(i, _):
                post(hop.at[step, hi], vcol.at[step, hi * Q + c_lo], VCOL, step, r_hi * Q + lax.rem(r_lo + i, Q), c_hi * Q + r_lo)
                return 0

            lax.fori_loop(0, Q, spread, 0)

    def multiply(step):
        with jax.named_scope("wait_vrow"):
            arrive(vrow, VROW, step)

        def transposed(n, _):
            acc = jnp.zeros((V, 2 * B), jnp.float32)
            for k in range(G // 2):
                v = jnp.concatenate([vrow[step, 2 * k], vrow[step, 2 * k + 1]], axis=1)
                w = tile[pl.ds(2 * k * B, 2 * B), pl.ds(pl.multiple_of(n * 2 * B, 2 * B), 2 * B)]
                acc += jnp.dot(v, w, preferred_element_type=jnp.float32)
            for u in range(2):
                j = 2 * n + u
                tsend[step, j] = acc[:, u * B : (u + 1) * B].astype(jnp.bfloat16)
                post(tsend.at[step, j], part.at[step, r_lo * Q + n // 2], PART, step, r_hi * Q + c_lo,
                     c_hi * Q + 2 * lax.rem(n, 2) + u)
            return 0

        with jax.named_scope("mm_transposed"):
            lax.fori_loop(0, G // 2, transposed, 0)

        with jax.named_scope("wait_vcol"):
            arrive(vcol, VCOL, step)

        def direct(i, _):
            n = lax.rem(2 * c_hi + Q + i, G // 2)
            acc = jnp.zeros((V, 2 * B), jnp.float32)
            for k in range(G // 2):
                v = jnp.concatenate([vcol[step, 2 * k], vcol[step, 2 * k + 1]], axis=1)
                w = tile[pl.ds(pl.multiple_of(n * 2 * B, 2 * B), 2 * B), pl.ds(2 * k * B, 2 * B)]
                acc += lax.dot_general(v, w, (((1,), (1,)), ((), ())), preferred_element_type=jnp.float32)
            for u in range(2):
                j = 2 * n + u
                dsend[step, j] = acc[:, u * B : (u + 1) * B].astype(jnp.bfloat16)
                post(dsend.at[step, j], drecv.at[step, c], DIRECT, step, r, j)
            return 0

        with jax.named_scope("mm_direct"):
            lax.fori_loop(0, G // 2, direct, 0)

    def collect(step):
        with jax.named_scope("wait_part"):
            arrive(part, PART, step)
        for k in range(Q):
            hi = lax.rem(c_hi + 2 + k, Q)
            total = jnp.zeros((V, B), jnp.float32)
            for lo in range(Q):
                total += part[step, lo * Q + hi].astype(jnp.float32)
            sums_send[step, k] = total.astype(jnp.bfloat16)
            post(sums_send.at[step, k], sums.at[step, r_hi], SUMS, step, c_hi * Q + r_lo, hi * Q + c_lo)
        applied = jnp.zeros((V, B), jnp.float32)
        with jax.named_scope("wait_drecv"):
            arrive(drecv, DIRECT, step)
        for k in range(G):
            applied += drecv[step, k].astype(jnp.float32)
        with jax.named_scope("wait_sums"):
            arrive(sums, SUMS, step)
        for k in range(Q):
            applied += sums[step, k].astype(jnp.float32)
        now = cur[...]
        mapped = scale_ref[...] * applied - center_shift * now
        factor = jnp.where(step == 0, 1.0 / half_width, 2.0 / half_width)
        updated = factor * mapped - prev[...]
        prev[...] = now
        cur[...] = updated

    def one_step(step, _):
        with jax.named_scope("share"):
            share(step)

        multiply(step)
        collect(step)
        return 0

    lax.fori_loop(0, STEPS, one_step, 0)
    out_ref[...] = cur[...]

    def drain(step, _):
        def sent(kind, buf, n):
            done = buf.at[step, pl.ds(0, n)]
            pltpu.make_async_copy(done, done, send_sem.at[kind, step]).wait()

        for kind, buf in ((VROW, vrow), (DIRECT, drecv)):
            sent(kind, buf, G - 1)
        for kind, buf, n, home, own in ((HOP, hop, Q, home_hi, 1), (SUMS, sums, Q, home_hi, 1), (VCOL, vcol, G, home_lo, Q),
                                        (PART, part, G, home_lo, Q)):
            sent(kind, buf, n - own)

            @pl.when(jnp.logical_not(home))
            def _():
                sent(kind, buf, own)

        return 0

    with jax.named_scope("drain"):
        lax.fori_loop(0, STEPS, drain, 0)


def per_device(start_vectors, scaling, block_values, block_places, block_counts):
    anywhere = pl.BlockSpec(memory_space=pl.ANY)

    def slab(n):
        return pltpu.VMEM((STEPS, n, V, B), jnp.bfloat16)

    f32 = pltpu.VMEM((V, B), jnp.float32)
    return pl.pallas_call(
        kernel,
        name="filter",
        out_shape=jax.ShapeDtypeStruct((V, B), jnp.float32),
        in_specs=[anywhere] * 5,
        out_specs=pl.BlockSpec(memory_space=pltpu.VMEM),
        scratch_shapes=[
            pltpu.VMEM((S + 1, B, B), jnp.bfloat16),
            pltpu.VMEM((G * B, G * B), jnp.bfloat16),
            f32,
            f32,
            pltpu.VMEM((1, B), jnp.float32),
            pltpu.VMEM((2, S), jnp.int32),
            pltpu.VMEM((1, 1), jnp.int32),
            pltpu.VMEM((2, S), jnp.int32),
            pltpu.SMEM((2, S), jnp.int32),
            pltpu.VMEM((STEPS, V, B), jnp.bfloat16),
            slab(Q), slab(G), slab(G), slab(G), slab(G), slab(G), slab(Q), slab(Q), slab(G),
            pltpu.SemaphoreType.DMA((6,)),
            pltpu.SemaphoreType.DMA((6, STEPS)),
            pltpu.SemaphoreType.DMA((6, STEPS)),
            pltpu.SemaphoreType.DMA((STEPS, Q)),
        ],
        compiler_params=pltpu.CompilerParams(collective_id=0, has_side_effects=True, vmem_limit_bytes=60 << 20),
    )(start_vectors, scaling.reshape(1, B), block_places.reshape(2, S), block_counts, block_values.reshape(S, B, B))


def solution(mesh):
    in_specs = (
        P(None, ("row", "col")),
        P(("row", "col")),
        P("row", "col", None, None, None),
        P("row", "col", None, None),
        P("row", "col"),
    )
    out_specs = P(None, ("row", "col"))
    return jax.shard_map(
        per_device, mesh=mesh, in_specs=in_specs, out_specs=out_specs, check_vma=False
    )
```

```python
import jax
import jax.numpy as jnp
from jax import lax
from jax.experimental import pallas as pl
from jax.experimental.pallas import tpu as pltpu
from jax.sharding import PartitionSpec as P

STEPS = 3
G = 16
Q = 4
B = 128
V = 64
S = 128
MESH = pl.DeviceIdType.MESH
VROW, HOP, VCOL, PART, SUMS, DIRECT, ROWX, EXCH = range(8)

center_shift = 0.5
half_width = 3.0


def kernel(x_hbm, scale_hbm, places_hbm, count_hbm, blocks_hbm, out_ref, blk, tile, cur, prev, scale_ref, places, count,
           table_v, table, piece, hop, row0, row1, row2, row3, col0, col1, col2, col3, tsend, dsend, part, sums_send, sums, drecv, in_sem, send_sem, recv_sem,
           hop_sem, row_sem, col_sem, mate_sem, exch_sem, acc, exch, dsum):
    vrow, vcol = (row0, row1, row2, row3), (col0, col1, col2, col3)
    r = lax.axis_index("row")
    c = lax.axis_index("col")
    r_hi, r_lo = r // Q, lax.rem(r, Q)
    c_hi, c_lo = c // Q, lax.rem(c, Q)
    home_hi, home_lo = r_hi == c_hi, r_lo == c_lo
    half, core = c // 2, lax.rem(c, 2)
    mate = c + 1 - 2 * core
    relay_lo = lax.rem(r_lo + Q - 1 + 2 * core, Q)
    origin_lo = lax.rem(r_lo + Q + 1 - 2 * core, Q)

    loads = [
        pltpu.make_async_copy(src, dst, in_sem.at[i])
        for i, (src, dst) in enumerate(((x_hbm, cur), (scale_hbm, scale_ref), (places_hbm, places), (count_hbm, count),
                                        (blocks_hbm, blk.at[pl.ds(0, S)])))
    ]
    for load in loads:
        load.start()

    barrier = pltpu.get_barrier_semaphore()

    def signal(row, col):
        pl.semaphore_signal(barrier, inc=1, device_id=(row, col), device_id_type=MESH)

    def greet_row(k, _):
        signal(r, lax.rem(c + k, G))
        return 0

    lax.fori_loop(1, G, greet_row, 0)

    def greet_near(k, _):
        signal(r_hi * Q + lax.rem(r_lo + 1 + k // Q, Q), c_hi * Q + lax.rem(k, Q))
        return 0

    lax.fori_loop(0, Q * (Q - 1), greet_near, 0)
    for k in range(1, Q):
        signal(lax.rem(r_hi + k, Q) * Q + relay_lo, r_hi * Q + c_lo)
        signal(c_hi * Q + origin_lo, lax.rem(c_hi + k, Q) * Q + c_lo)
        signal(lax.rem(r_hi + k, Q) * Q + r_lo, r_hi * Q + c_lo)

    @pl.when(jnp.logical_not(home_hi))
    def _():
        signal(r_hi * Q + relay_lo, r_hi * Q + c_lo)
        signal(c_hi * Q + origin_lo, c_hi * Q + c_lo)
        for k in range(1, Q):
            signal(c_hi * Q + r_lo, lax.rem(r_hi + k, Q) * Q + c_lo)

    prev[...] = jnp.zeros((V, B), jnp.float32)
    blk[S] = jnp.zeros((B, B), jnp.bfloat16)

    loads[2].wait()
    loads[3].wait()
    lane = lax.broadcasted_iota(jnp.int32, (1, S), 1)
    at = jnp.where(lane < count[...], places[0:1, :] * G + places[1:2, :], -1)
    row_id = lax.broadcasted_iota(jnp.int32, (S, S), 0)
    col_id = lax.broadcasted_iota(jnp.int32, (S, S), 1)
    for upper in range(2):
        slot = jnp.min(jnp.where(row_id + upper * S == at, col_id, S), axis=1, keepdims=True)
        table_v[upper : upper + 1, :] = jnp.min(jnp.where(row_id == col_id, slot, S), axis=0, keepdims=True)
    to_scalars = pltpu.make_async_copy(table_v, table, in_sem.at[5])
    to_scalars.start()
    loads[0].wait()
    loads[1].wait()
    with jax.named_scope("load"):
        loads[4].wait()
        to_scalars.wait()

    def build(i, _):
        for j in range(G):
            slot = jnp.clip(table[i // 8, lax.rem(i, 8) * G + j], 0, S)
            tile[pl.ds(pl.multiple_of(i * B, B), B), pl.ds(j * B, B)] = blk[slot]
        return 0

    with jax.named_scope("build"):
        lax.fori_loop(0, G, build, 0)

    with jax.named_scope("barrier"):
        pl.semaphore_wait(barrier, G - 1 + Q * (Q - 1) + jnp.where(home_hi, 9, 14))

    def post(src, dst, kind, step, row, col, arrival=None):
        own = jnp.logical_and(row == r, col == c)
        arrival = recv_sem.at[kind, step] if arrival is None else arrival

        @pl.when(own)
        def _():
            pltpu.make_async_copy(src, dst, arrival).start()

        @pl.when(jnp.logical_not(own))
        def _():
            pltpu.make_async_remote_copy(src, dst, send_sem.at[kind, step], arrival, device_id=(row, col),
                                         device_id_type=MESH).start()

    def to_mate(src, dst, kind, step, arrival):
        pltpu.make_async_remote_copy(src, dst, send_sem.at[kind, step], arrival, device_id=(r, mate),
                                     device_id_type=MESH).start()

    def arrive(buf, kind, step):
        pltpu.make_async_copy(buf.at[step], buf.at[step], recv_sem.at[kind, step]).wait()

    def share(step):
        piece[step] = (scale_ref[...] * cur[...]).astype(jnp.bfloat16)

        for k in (2, 1, 3, 0):
            row, col = lax.rem(r_hi + k, Q) * Q + relay_lo, r_hi * Q + c_lo
            post(piece.at[step], hop.at[step, c_hi], HOP, step, row, col, hop_sem.at[step, c_hi])
        for k in (2, 1, 3, 0):
            hi = lax.rem(c_hi + k, Q)

            for i in range(2):
                post(piece.at[step], vrow[(Q - k) % Q].at[step, 2 * core + c_lo // 2], VROW, step, r, hi * Q + 2 * i + core,
                     row_sem.at[step, (Q - k) % Q])
        for k in (0, 1, 3, 2):
            pair = vrow[k].at[step, pl.ds(2 * core, 2)]
            pltpu.make_async_copy(pair, pair, row_sem.at[step, k]).wait()
            for i in range(2):
                both = vrow[k].at[step, 2 * core + i]
                to_mate(both, both, ROWX, step, mate_sem.at[step, k])
        for k in (0, 1, 3, 2):
            hi = lax.rem(c_hi + k, Q)
            pltpu.make_async_copy(hop.at[step, hi], hop.at[step, hi], hop_sem.at[step, hi]).wait()

            def spread(i, _):
                post(hop.at[step, hi], vcol[k].at[step, c_lo], VCOL, step, r_hi * Q + lax.rem(r_lo + i, Q), c_hi * Q + origin_lo,
                     col_sem.at[step, k])
                return 0

            lax.fori_loop(0, Q, spread, 0)

    def multiply(step, buf, sem, awaited, order, block, name, last, emit):
        for at, k in enumerate((0, 1, 3, 2)):
            hi = lax.rem(c_hi + k, Q)
            pieces = buf[k].at[step, awaited]
            with jax.named_scope("wait_" + name):
                pltpu.make_async_copy(pieces, pieces, sem.at[step, k]).wait()

            def term(n):
                v = jnp.concatenate([buf[k][step, u] for u in order], axis=1)
                total = block(v, pl.ds(pl.multiple_of(hi * Q * B, Q * B), Q * B), pl.ds(n * 2 * B, 2 * B))
                if at:
                    total += acc[n]
                if at < Q - 1:
                    acc[n] = total
                else:
                    last(n, total)

            with jax.named_scope("mm_" + name):
                for part_of in range(2):
                    for n in range(part_of * Q, part_of * Q + Q):
                        term(n)
                    if at == Q - 1:
                        emit(part_of)

    def transposed(step):
        def block(v, inner, outer):
            return jnp.dot(v, tile[inner, outer], preferred_element_type=jnp.float32)

        def last(n, total):
            for u in range(2):
                tsend[step, 2 * n + u] = total[:, u * B : (u + 1) * B].astype(jnp.bfloat16)

        def emit(part_of):
            def send(j, _):
                post(tsend.at[step, j], part.at[step, r_lo * Q + j // Q], PART, step, r_hi * Q + c_lo, c_hi * Q + lax.rem(j, Q))
                return 0

            lax.fori_loop(part_of * 2 * Q, part_of * 2 * Q + 2 * Q, send, 0)

        multiply(step, vrow, mate_sem, pl.ds(2 - 2 * core, 2), (0, 2, 1, 3), block, "row", last, emit)

    def meet(step):
        with jax.named_scope("wait_part"):
            arrive(part, PART, step)
        for k in range(Q):
            hi = lax.rem(c_hi + 2 + k, Q)
            total = jnp.zeros((V, B), jnp.float32)
            for lo in range(Q):
                total += part[step, lo * Q + hi].astype(jnp.float32)
            sums_send[step, k] = total.astype(jnp.bfloat16)
            post(sums_send.at[step, k], sums.at[step, r_hi], SUMS, step, c_hi * Q + r_lo, hi * Q + c_lo)

    def direct(step):
        def block(v, inner, outer):
            return lax.dot_general(v, tile[outer, inner], (((1,), (1,)), ((), ())), preferred_element_type=jnp.float32)

        def last(n, total):
            acc[n] = total
            dsend[step, n] = acc[n, :, pl.ds(pl.multiple_of((1 - core) * B, B), B)].astype(jnp.bfloat16)

        def emit(part_of):
            for n in range(part_of * Q, part_of * Q + Q):
                to_mate(dsend.at[step, n], exch.at[step, n], EXCH, step, exch_sem.at[step, part_of])

        multiply(step, vcol, col_sem, pl.ds(0, Q), range(Q), block, "col", last, emit)
        meet(step)
        for part_of in range(2):
            mine = exch.at[step, pl.ds(part_of * Q, Q)]
            with jax.named_scope("wait_mate"):
                pltpu.make_async_copy(mine, mine, exch_sem.at[step, part_of]).wait()
            for n in range(part_of * Q, part_of * Q + Q):
                own = acc[n, :, pl.ds(pl.multiple_of(core * B, B), B)]
                dsum[step, n] = (own + exch[step, n].astype(jnp.float32)).astype(jnp.bfloat16)

        def send(i, _):
            n = lax.rem(half + Q + i, G // 2)
            post(dsum.at[step, n], drecv.at[step, half], DIRECT, step, r, 2 * n + core)
            return 0

        lax.fori_loop(0, G // 2, send, 0)

    def collect(step):
        applied = jnp.zeros((V, B), jnp.float32)
        with jax.named_scope("wait_drecv"):
            arrive(drecv, DIRECT, step)
        for k in range(G // 2):
            applied += drecv[step, k].astype(jnp.float32)
        with jax.named_scope("wait_sums"):
            arrive(sums, SUMS, step)
        for k in range(Q):
            applied += sums[step, k].astype(jnp.float32)
        now = cur[...]
        mapped = scale_ref[...] * applied - center_shift * now
        factor = jnp.where(step == 0, 1.0 / half_width, 2.0 / half_width)
        updated = factor * mapped - prev[...]
        prev[...] = now
        cur[...] = updated

    def one_step(step, _):
        with jax.named_scope("share"):
            share(step)

        transposed(step)
        direct(step)
        collect(step)
        return 0

    lax.fori_loop(0, STEPS, one_step, 0)
    out_ref[...] = cur[...]

    def drain(step, _):
        def sent(kind, buf, n):
            done = buf.at[step, pl.ds(0, n)]
            pltpu.make_async_copy(done, done, send_sem.at[kind, step]).wait()

        for kind, n in ((VROW, G // 2 - 1), (DIRECT, G // 2 - 1), (ROWX, G // 2), (EXCH, G // 2)):
            sent(kind, part, n)
        sent(HOP, hop, Q)
        for kind, buf, n, home, own in ((SUMS, sums, Q, home_hi, 1), (VCOL, part, G, origin_lo == c_lo, Q),
                                        (PART, part, G, home_lo, Q)):
            sent(kind, buf, n - own)

            @pl.when(jnp.logical_not(home))
            def _():
                sent(kind, buf, own)

        return 0

    with jax.named_scope("drain"):
        lax.fori_loop(0, STEPS, drain, 0)


def per_device(start_vectors, scaling, block_values, block_places, block_counts):
    anywhere = pl.BlockSpec(memory_space=pl.ANY)

    def slab(n):
        return pltpu.VMEM((STEPS, n, V, B), jnp.bfloat16)

    f32 = pltpu.VMEM((V, B), jnp.float32)
    return pl.pallas_call(
        kernel,
        name="filter",
        out_shape=jax.ShapeDtypeStruct((V, B), jnp.float32),
        in_specs=[anywhere] * 5,
        out_specs=pl.BlockSpec(memory_space=pltpu.VMEM),
        scratch_shapes=[
            pltpu.VMEM((S + 1, B, B), jnp.bfloat16),
            pltpu.VMEM((G * B, G * B), jnp.bfloat16),
            f32,
            f32,
            pltpu.VMEM((1, B), jnp.float32),
            pltpu.VMEM((2, S), jnp.int32),
            pltpu.VMEM((1, 1), jnp.int32),
            pltpu.VMEM((2, S), jnp.int32),
            pltpu.SMEM((2, S), jnp.int32),
            pltpu.VMEM((STEPS, V, B), jnp.bfloat16),
            slab(Q), *[slab(Q)] * 8, slab(G), slab(G // 2), slab(G), slab(Q), slab(Q), slab(G // 2),
            pltpu.SemaphoreType.DMA((6,)),
            pltpu.SemaphoreType.DMA((8, STEPS)),
            pltpu.SemaphoreType.DMA((8, STEPS)),
            pltpu.SemaphoreType.DMA((STEPS, Q)),
            pltpu.SemaphoreType.DMA((STEPS, Q)),
            pltpu.SemaphoreType.DMA((STEPS, Q)),
            pltpu.SemaphoreType.DMA((STEPS, Q)),
            pltpu.SemaphoreType.DMA((STEPS, 2)),
            pltpu.VMEM((G // 2, V, 2 * B), jnp.float32),
            slab(G // 2), slab(G // 2),
        ],
        compiler_params=pltpu.CompilerParams(collective_id=0, has_side_effects=True, vmem_limit_bytes=60 << 20),
    )(start_vectors, scaling.reshape(1, B), block_places.reshape(2, S), block_counts, block_values.reshape(S, B, B))


def solution(mesh):
    in_specs = (
        P(None, ("row", "col")),
        P(("row", "col")),
        P("row", "col", None, None, None),
        P("row", "col", None, None),
        P("row", "col"),
    )
    out_specs = P(None, ("row", "col"))
    return jax.shard_map(
        per_device, mesh=mesh, in_specs=in_specs, out_specs=out_specs, check_vma=False
    )
```

```python
import jax
import jax.numpy as jnp
from jax import lax
from jax.experimental import pallas as pl
from jax.experimental.pallas import tpu as pltpu
from jax.sharding import PartitionSpec as P

STEPS = 3
G = 16
Q = 4
B = 128
V = 64
S = 128
MESH = pl.DeviceIdType.MESH
VROW, HOP, VCOL, PART, SUMS, DIRECT, ROWX, EXCH = range(8)

center_shift = 0.5
half_width = 3.0


def kernel(x_hbm, scale_hbm, places_hbm, count_hbm, blocks_hbm, out_ref, blk, tile, cur, prev, scale_ref, places, count,
           table_v, table, piece, hop, row0, row1, row2, row3, col0, col1, col2, col3, tsend, dsend, part, sums_send, sums, drecv, in_sem, send_sem, recv_sem,
           hop_sem, row_sem, col_sem, mate_sem, exch_sem, acc, exch, dsum):
    vrow, vcol = (row0, row1, row2, row3), (col0, col1, col2, col3)
    r = lax.axis_index("row")
    c = lax.axis_index("col")
    r_hi, r_lo = r // Q, lax.rem(r, Q)
    c_hi, c_lo = c // Q, lax.rem(c, Q)
    home_hi, home_lo = r_hi == c_hi, r_lo == c_lo
    half, core = c // 2, lax.rem(c, 2)
    mate = c + 1 - 2 * core
    relay_lo = lax.rem(r_lo + Q - 1 + 2 * core, Q)
    origin_lo = lax.rem(r_lo + Q + 1 - 2 * core, Q)

    loads = [
        pltpu.make_async_copy(src, dst, in_sem.at[i])
        for i, (src, dst) in enumerate(((x_hbm, cur), (scale_hbm, scale_ref), (places_hbm, places), (count_hbm, count),
                                        (blocks_hbm, blk.at[pl.ds(0, S)])))
    ]
    for load in loads:
        load.start()

    barrier = pltpu.get_barrier_semaphore()

    def signal(row, col):
        pl.semaphore_signal(barrier, inc=1, device_id=(row, col), device_id_type=MESH)

    for k in range(1, Q):
        signal(lax.rem(r_hi + k, Q) * Q + relay_lo, r_hi * Q + c_lo)
        signal(c_hi * Q + origin_lo, lax.rem(c_hi + k, Q) * Q + c_lo)
        signal(lax.rem(r_hi + k, Q) * Q + r_lo, r_hi * Q + c_lo)

    @pl.when(jnp.logical_not(home_hi))
    def _():
        signal(r_hi * Q + relay_lo, r_hi * Q + c_lo)
        signal(c_hi * Q + origin_lo, c_hi * Q + c_lo)
        for k in range(1, Q):
            signal(c_hi * Q + r_lo, lax.rem(r_hi + k, Q) * Q + c_lo)

    def greet_row(k, _):
        signal(r, lax.rem(c + k, G))
        return 0

    lax.fori_loop(1, G, greet_row, 0)

    def greet_near(k, _):
        signal(r_hi * Q + lax.rem(r_lo + 1 + k // Q, Q), c_hi * Q + lax.rem(k, Q))
        return 0

    lax.fori_loop(0, Q * (Q - 1), greet_near, 0)
    prev[...] = jnp.zeros((V, B), jnp.float32)
    blk[S] = jnp.zeros((B, B), jnp.bfloat16)

    loads[2].wait()
    loads[3].wait()
    lane = lax.broadcasted_iota(jnp.int32, (1, S), 1)
    at = jnp.where(lane < count[...], places[0:1, :] * G + places[1:2, :], -1)
    row_id = lax.broadcasted_iota(jnp.int32, (S, S), 0)
    col_id = lax.broadcasted_iota(jnp.int32, (S, S), 1)
    for upper in range(2):
        slot = jnp.min(jnp.where(row_id + upper * S == at, col_id, S), axis=1, keepdims=True)
        table_v[upper : upper + 1, :] = jnp.min(jnp.where(row_id == col_id, slot, S), axis=0, keepdims=True)
    to_scalars = pltpu.make_async_copy(table_v, table, in_sem.at[5])
    to_scalars.start()
    loads[0].wait()
    loads[1].wait()
    def build(i, _):
        for j in range(G):
            slot = jnp.clip(table[i // 8, lax.rem(i, 8) * G + j], 0, S)
            tile[pl.ds(pl.multiple_of(i * B, B), B), pl.ds(j * B, B)] = blk[slot]
        return 0

    with jax.named_scope("barrier"):
        pl.semaphore_wait(barrier, G - 1 + Q * (Q - 1) + jnp.where(home_hi, 9, 14))

    def push(src, dst, kind, step, row, col, arrival):
        pltpu.make_async_remote_copy(src, dst, send_sem.at[kind, step], arrival, device_id=(row, col), device_id_type=MESH).start()

    def post(src, dst, kind, step, row, col, arrival, own):
        if own is True:
            pltpu.make_async_copy(src, dst, arrival).start()
            return

        @pl.when(own)
        def _():
            pltpu.make_async_copy(src, dst, arrival).start()

        @pl.when(jnp.logical_not(own))
        def _():
            push(src, dst, kind, step, row, col, arrival)

    def to_mate(src, dst, kind, step, arrival):
        pltpu.make_async_remote_copy(src, dst, send_sem.at[kind, step], arrival, device_id=(r, mate),
                                     device_id_type=MESH).start()

    def arrive(buf, kind, step):
        pltpu.make_async_copy(buf.at[step], buf.at[step], recv_sem.at[kind, step]).wait()

    def share(step):
        piece[step] = (scale_ref[...] * cur[...]).astype(jnp.bfloat16)

        for k in (2, 1, 3, 0):
            row, col = lax.rem(r_hi + k, Q) * Q + relay_lo, r_hi * Q + c_lo
            push(piece.at[step], hop.at[step, c_hi], HOP, step, row, col, hop_sem.at[step, c_hi])
        for k in (2, 1, 3, 0):
            hi = lax.rem(c_hi + k, Q)

            for i in range(2):
                there, arrival = vrow[(Q - k) % Q].at[step, 2 * core + c_lo // 2], row_sem.at[step, (Q - k) % Q]
                col = hi * Q + 2 * lax.rem(c_lo // 2 + 1 - i, 2) + core
                if k or not i:
                    push(piece.at[step], there, VROW, step, r, col, arrival)
                else:
                    post(piece.at[step], there, VROW, step, r, col, arrival, True)

    def hand_over(step):
        for k in (0, 1, 3, 2):
            pair = vrow[k].at[step, pl.ds(2 * core, 2)]
            pltpu.make_async_copy(pair, pair, row_sem.at[step, k]).wait()
            for i in range(2):
                both = vrow[k].at[step, 2 * core + i]
                to_mate(both, both, ROWX, step, mate_sem.at[step, k])

    def relay(step):
        for k in (0, 1, 3, 2):
            hi = lax.rem(c_hi + k, Q)
            pltpu.make_async_copy(hop.at[step, hi], hop.at[step, hi], hop_sem.at[step, hi]).wait()

            for i in (2, 1, 3, 0):
                row, col = r_hi * Q + lax.rem(r_lo + i, Q), c_hi * Q + origin_lo
                if i:
                    push(hop.at[step, hi], vcol[k].at[step, c_lo], VCOL, step, row, col, col_sem.at[step, k])
                else:
                    post(hop.at[step, hi], vcol[k].at[step, c_lo], VCOL, step, row, col, col_sem.at[step, k], origin_lo == c_lo)

    def multiply(step, buf, sem, awaited, order, block, name, last, emit):
        for at, k in enumerate((0, 1, 3, 2)):
            hi = lax.rem(c_hi + k, Q)
            pieces = buf[k].at[step, awaited]
            with jax.named_scope("wait_" + name):
                pltpu.make_async_copy(pieces, pieces, sem.at[step, k]).wait()

            def term(n):
                v = jnp.concatenate([buf[k][step, u] for u in order], axis=1)
                total = block(v, pl.ds(pl.multiple_of(hi * Q * B, Q * B), Q * B), pl.ds(n * 2 * B, 2 * B))
                if at:
                    total += acc[n]
                if at < Q - 1:
                    acc[n] = total
                else:
                    last(n, total)

            with jax.named_scope("mm_" + name):
                for part_of in range(2):
                    for n in range(part_of * Q, part_of * Q + Q):
                        term(n)
                    if at == Q - 1:
                        emit(part_of)

    def transposed(step):
        def block(v, inner, outer):
            return jnp.dot(v, tile[inner, outer], preferred_element_type=jnp.float32)

        def last(n, total):
            for u in range(2):
                tsend[step, 2 * n + u] = total[:, u * B : (u + 1) * B].astype(jnp.bfloat16)

        def emit(part_of):
            for y in range(2 * part_of, 2 * part_of + 2):
                for i in range(Q):
                    lo = lax.rem(c_lo + i, Q)
                    src, dst = tsend.at[step, y * Q + lo], part.at[step, r_lo * Q + y]
                    row, col = r_hi * Q + c_lo, c_hi * Q + lo
                    if i:
                        push(src, dst, PART, step, row, col, recv_sem.at[PART, step])
                    else:
                        post(src, dst, PART, step, row, col, recv_sem.at[PART, step], home_lo)

        multiply(step, vrow, mate_sem, pl.ds(2 - 2 * core, 2), (0, 2, 1, 3), block, "row", last, emit)

    def meet(step):
        with jax.named_scope("wait_part"):
            arrive(part, PART, step)
        for k in range(Q):
            hi = lax.rem(c_hi + 2 + k, Q)
            total = jnp.zeros((V, B), jnp.float32)
            for lo in range(Q):
                total += part[step, lo * Q + hi].astype(jnp.float32)
            sums_send[step, k] = total.astype(jnp.bfloat16)
            row, col, arrival = c_hi * Q + r_lo, hi * Q + c_lo, recv_sem.at[SUMS, step]
            if k != 2:
                push(sums_send.at[step, k], sums.at[step, r_hi], SUMS, step, row, col, arrival)
            else:
                post(sums_send.at[step, k], sums.at[step, r_hi], SUMS, step, row, col, arrival, home_hi)

    def direct(step):
        def block(v, inner, outer):
            return lax.dot_general(v, tile[outer, inner], (((1,), (1,)), ((), ())), preferred_element_type=jnp.float32)

        def last(n, total):
            acc[n] = total
            dsend[step, n] = acc[n, :, pl.ds(pl.multiple_of((1 - core) * B, B), B)].astype(jnp.bfloat16)

        def emit(part_of):
            for n in range(part_of * Q, part_of * Q + Q):
                to_mate(dsend.at[step, n], exch.at[step, n], EXCH, step, exch_sem.at[step, part_of])

        multiply(step, vcol, col_sem, pl.ds(0, Q), range(Q), block, "col", last, emit)
        meet(step)
        for part_of in range(2):
            mine = exch.at[step, pl.ds(part_of * Q, Q)]
            with jax.named_scope("wait_mate"):
                pltpu.make_async_copy(mine, mine, exch_sem.at[step, part_of]).wait()
            for n in range(part_of * Q, part_of * Q + Q):
                own = acc[n, :, pl.ds(pl.multiple_of(core * B, B), B)]
                dsum[step, n] = (own + exch[step, n].astype(jnp.float32)).astype(jnp.bfloat16)

        for i in range(G // 2):
            n = lax.rem(half + Q + i, G // 2)
            src, dst, arrival = dsum.at[step, n], drecv.at[step, half], recv_sem.at[DIRECT, step]
            if i != Q:
                push(src, dst, DIRECT, step, r, 2 * n + core, arrival)
            else:
                post(src, dst, DIRECT, step, r, 2 * n + core, arrival, True)

    def collect(step):
        applied = jnp.zeros((V, B), jnp.float32)
        with jax.named_scope("wait_drecv"):
            arrive(drecv, DIRECT, step)
        for k in range(G // 2):
            applied += drecv[step, k].astype(jnp.float32)
        with jax.named_scope("wait_sums"):
            arrive(sums, SUMS, step)
        for k in range(Q):
            applied += sums[step, k].astype(jnp.float32)
        now = cur[...]
        mapped = scale_ref[...] * applied - center_shift * now
        factor = jnp.where(step == 0, 1.0 / half_width, 2.0 / half_width)
        updated = factor * mapped - prev[...]
        prev[...] = now
        cur[...] = updated

    def one_step(step, _):
        share(step)

        @pl.when(step == 0)
        def _():
            with jax.named_scope("build"):
                loads[4].wait()
                to_scalars.wait()
                lax.fori_loop(0, G, build, 0)

        with jax.named_scope("hand_over"):
            hand_over(step)
        with jax.named_scope("relay"):
            relay(step)
        transposed(step)
        direct(step)
        collect(step)
        return 0

    lax.fori_loop(0, STEPS, one_step, 0)
    out_ref[...] = cur[...]

    def drain(step, _):
        def sent(kind, buf, n):
            done = buf.at[step, pl.ds(0, n)]
            pltpu.make_async_copy(done, done, send_sem.at[kind, step]).wait()

        for kind, n in ((VROW, G // 2 - 1), (DIRECT, G // 2 - 1), (ROWX, G // 2), (EXCH, G // 2)):
            sent(kind, part, n)
        sent(HOP, hop, Q)
        for kind, buf, n, home, own in ((SUMS, sums, Q, home_hi, 1), (VCOL, part, G, origin_lo == c_lo, Q),
                                        (PART, part, G, home_lo, Q)):
            sent(kind, buf, n - own)

            @pl.when(jnp.logical_not(home))
            def _():
                sent(kind, buf, own)

        return 0

    with jax.named_scope("drain"):
        lax.fori_loop(0, STEPS, drain, 0)


def per_device(start_vectors, scaling, block_values, block_places, block_counts):
    anywhere = pl.BlockSpec(memory_space=pl.ANY)

    def slab(n):
        return pltpu.VMEM((STEPS, n, V, B), jnp.bfloat16)

    f32 = pltpu.VMEM((V, B), jnp.float32)
    return pl.pallas_call(
        kernel,
        name="filter",
        out_shape=jax.ShapeDtypeStruct((V, B), jnp.float32),
        in_specs=[anywhere] * 5,
        out_specs=pl.BlockSpec(memory_space=pltpu.VMEM),
        scratch_shapes=[
            pltpu.VMEM((S + 1, B, B), jnp.bfloat16),
            pltpu.VMEM((G * B, G * B), jnp.bfloat16),
            f32,
            f32,
            pltpu.VMEM((1, B), jnp.float32),
            pltpu.VMEM((2, S), jnp.int32),
            pltpu.VMEM((1, 1), jnp.int32),
            pltpu.VMEM((2, S), jnp.int32),
            pltpu.SMEM((2, S), jnp.int32),
            pltpu.VMEM((STEPS, V, B), jnp.bfloat16),
            slab(Q), *[slab(Q)] * 8, slab(G), slab(G // 2), slab(G), slab(Q), slab(Q), slab(G // 2),
            pltpu.SemaphoreType.DMA((6,)),
            pltpu.SemaphoreType.DMA((8, STEPS)),
            pltpu.SemaphoreType.DMA((8, STEPS)),
            pltpu.SemaphoreType.DMA((STEPS, Q)),
            pltpu.SemaphoreType.DMA((STEPS, Q)),
            pltpu.SemaphoreType.DMA((STEPS, Q)),
            pltpu.SemaphoreType.DMA((STEPS, Q)),
            pltpu.SemaphoreType.DMA((STEPS, 2)),
            pltpu.VMEM((G // 2, V, 2 * B), jnp.float32),
            slab(G // 2), slab(G // 2),
        ],
        compiler_params=pltpu.CompilerParams(collective_id=0, has_side_effects=True, vmem_limit_bytes=60 << 20),
    )(start_vectors, scaling.reshape(1, B), block_places.reshape(2, S), block_counts, block_values.reshape(S, B, B))


def solution(mesh):
    in_specs = (
        P(None, ("row", "col")),
        P(("row", "col")),
        P("row", "col", None, None, None),
        P("row", "col", None, None),
        P("row", "col"),
    )
    out_specs = P(None, ("row", "col"))
    return jax.shard_map(
        per_device, mesh=mesh, in_specs=in_specs, out_specs=out_specs, check_vma=False
    )
```

```python
import jax
import jax.numpy as jnp
from jax import lax
from jax.experimental import pallas as pl
from jax.experimental.pallas import tpu as pltpu
from jax.sharding import PartitionSpec as P

STEPS = 3
G = 16
Q = 4
B = 128
V = 64
S = 128
MESH = pl.DeviceIdType.MESH
VROW, HOP, VCOL, PART, SUMS, DIRECT, ROWX, EXCH = range(8)

center_shift = 0.5
half_width = 3.0


def kernel(x_hbm, scale_hbm, places_hbm, count_hbm, blocks_hbm, out_ref, blk, tile, cur, prev, scale_ref, places, count,
           table_v, table, piece, hop, row0, row1, row2, row3, col0, col1, col2, col3, tsend, dsend, part, sums_send, sums, drecv, in_sem, send_sem, recv_sem,
           hop_sem, row_sem, col_sem, mate_sem, exch_sem, acc, exch, dsum):
    vrow, vcol = (row0, row1, row2, row3), (col0, col1, col2, col3)
    r = lax.axis_index("row")
    c = lax.axis_index("col")
    r_hi, r_lo = r // Q, lax.rem(r, Q)
    c_hi, c_lo = c // Q, lax.rem(c, Q)
    home_hi, home_lo = r_hi == c_hi, r_lo == c_lo
    half, core = c // 2, lax.rem(c, 2)
    mate = c + 1 - 2 * core
    relay_lo = lax.rem(r_lo + Q - 1 + 2 * core, Q)
    origin_lo = lax.rem(r_lo + Q + 1 - 2 * core, Q)

    loads = [
        pltpu.make_async_copy(src, dst, in_sem.at[i])
        for i, (src, dst) in enumerate(((x_hbm, cur), (scale_hbm, scale_ref), (places_hbm, places), (count_hbm, count),
                                        (blocks_hbm, blk.at[pl.ds(0, S)])))
    ]
    for load in loads:
        load.start()

    barrier = pltpu.get_barrier_semaphore()

    def signal(row, col):
        pl.semaphore_signal(barrier, inc=1, device_id=(row, col), device_id_type=MESH)

    for k in range(1, Q):
        signal(lax.rem(r_hi + k, Q) * Q + relay_lo, r_hi * Q + c_lo)
        signal(c_hi * Q + origin_lo, lax.rem(c_hi + k, Q) * Q + c_lo)
        signal(lax.rem(r_hi + k, Q) * Q + r_lo, r_hi * Q + c_lo)

    @pl.when(jnp.logical_not(home_hi))
    def _():
        signal(r_hi * Q + relay_lo, r_hi * Q + c_lo)
        signal(c_hi * Q + origin_lo, c_hi * Q + c_lo)
        for k in range(1, Q):
            signal(c_hi * Q + r_lo, lax.rem(r_hi + k, Q) * Q + c_lo)

    def greet_row(k, _):
        signal(r, lax.rem(c + k, G))
        return 0

    lax.fori_loop(1, G, greet_row, 0)

    def greet_near(k, _):
        signal(r_hi * Q + lax.rem(r_lo + 1 + k // Q, Q), c_hi * Q + lax.rem(k, Q))
        return 0

    lax.fori_loop(0, Q * (Q - 1), greet_near, 0)
    prev[...] = jnp.zeros((V, B), jnp.float32)
    blk[S] = jnp.zeros((B, B), jnp.bfloat16)

    loads[2].wait()
    loads[3].wait()
    lane = lax.broadcasted_iota(jnp.int32, (1, S), 1)
    at = jnp.where(lane < count[...], places[0:1, :] * G + places[1:2, :], -1)
    row_id = lax.broadcasted_iota(jnp.int32, (S, S), 0)
    col_id = lax.broadcasted_iota(jnp.int32, (S, S), 1)
    for upper in range(2):
        slot = jnp.min(jnp.where(row_id + upper * S == at, col_id, S), axis=1, keepdims=True)
        table_v[upper : upper + 1, :] = jnp.min(jnp.where(row_id == col_id, slot, S), axis=0, keepdims=True)
    to_scalars = pltpu.make_async_copy(table_v, table, in_sem.at[5])
    to_scalars.start()
    loads[0].wait()
    loads[1].wait()
    def build(i, _):
        for j in range(G):
            slot = jnp.clip(table[i // 8, lax.rem(i, 8) * G + j], 0, S)
            tile[pl.ds(pl.multiple_of(i * B, B), B), pl.ds(j * B, B)] = blk[slot]
        return 0

    with jax.named_scope("barrier"):
        pl.semaphore_wait(barrier, G - 1 + Q * (Q - 1) + jnp.where(home_hi, 9, 14))

    def push(src, dst, kind, step, row, col, arrival):
        pltpu.make_async_remote_copy(src, dst, send_sem.at[kind, step], arrival, device_id=(row, col), device_id_type=MESH).start()

    def post(src, dst, kind, step, row, col, arrival, own):
        if own is True:
            pltpu.make_async_copy(src, dst, arrival).start()
            return

        @pl.when(own)
        def _():
            pltpu.make_async_copy(src, dst, arrival).start()

        @pl.when(jnp.logical_not(own))
        def _():
            push(src, dst, kind, step, row, col, arrival)

    def to_mate(src, dst, kind, step, arrival):
        pltpu.make_async_remote_copy(src, dst, send_sem.at[kind, step], arrival, device_id=(r, mate),
                                     device_id_type=MESH).start()

    def arrive(buf, kind, step):
        pltpu.make_async_copy(buf.at[step], buf.at[step], recv_sem.at[kind, step]).wait()

    def share(step):
        piece[step] = (scale_ref[...] * cur[...]).astype(jnp.bfloat16)

        for k in (2, 1, 3, 0):
            row, col = lax.rem(r_hi + k, Q) * Q + relay_lo, r_hi * Q + c_lo
            push(piece.at[step], hop.at[step, c_hi], HOP, step, row, col, hop_sem.at[step, c_hi])
        for k in (2, 1, 3, 0):
            hi = lax.rem(c_hi + k, Q)

            for i in range(2):
                there, arrival = vrow[(Q - k) % Q].at[step, 2 * core + c_lo // 2], row_sem.at[step, (Q - k) % Q]
                col = hi * Q + 2 * lax.rem(c_lo // 2 + 1 - i, 2) + core
                if k or not i:
                    push(piece.at[step], there, VROW, step, r, col, arrival)
                else:
                    post(piece.at[step], there, VROW, step, r, col, arrival, True)

    def hand_over(step):
        for k in (0, 1, 3, 2):
            pair = vrow[k].at[step, pl.ds(2 * core, 2)]
            pltpu.make_async_copy(pair, pair, row_sem.at[step, k]).wait()
            for i in range(2):
                both = vrow[k].at[step, 2 * core + i]
                to_mate(both, both, ROWX, step, mate_sem.at[step, k])

    def relay(step):
        for k in (0, 1, 3, 2):
            hi = lax.rem(c_hi + k, Q)
            pltpu.make_async_copy(hop.at[step, hi], hop.at[step, hi], hop_sem.at[step, hi]).wait()

            for i in (2, 1, 3, 0):
                row, col = r_hi * Q + lax.rem(r_lo + i, Q), c_hi * Q + origin_lo
                if i:
                    push(hop.at[step, hi], vcol[k].at[step, c_lo], VCOL, step, row, col, col_sem.at[step, k])
                else:
                    post(hop.at[step, hi], vcol[k].at[step, c_lo], VCOL, step, row, col, col_sem.at[step, k], origin_lo == c_lo)

    def multiply(step, buf, sem, awaited, order, block, name, last, emit):
        for at, k in enumerate((0, 1, 3, 2)):
            hi = lax.rem(c_hi + k, Q)
            pieces = buf[k].at[step, awaited]
            with jax.named_scope("wait_" + name):
                pltpu.make_async_copy(pieces, pieces, sem.at[step, k]).wait()

            def term(n):
                v = jnp.concatenate([buf[k][step, u] for u in order], axis=1)
                total = block(v, pl.ds(pl.multiple_of(hi * Q * B, Q * B), Q * B), pl.ds(n * 2 * B, 2 * B))
                if at:
                    total += acc[n]
                if at < Q - 1:
                    acc[n] = total
                else:
                    last(n, total)

            with jax.named_scope("mm_" + name):
                for part_of in range(2):
                    for n in range(part_of * Q, part_of * Q + Q):
                        term(n)
                    if at == Q - 1:
                        emit(part_of)

    def transposed(step):
        def block(v, inner, outer):
            return jnp.dot(v, tile[inner, outer], preferred_element_type=jnp.float32)

        def last(n, total):
            for u in range(2):
                tsend[step, 2 * n + u] = total[:, u * B : (u + 1) * B].astype(jnp.bfloat16)

        def emit(y):
            for i in range(Q):
                lo = lax.rem(c_lo + i, Q)
                src, dst = tsend.at[step, y * Q + lo], part.at[step, r_lo * Q + y]
                row, col = r_hi * Q + c_lo, c_hi * Q + lo
                if i:
                    push(src, dst, PART, step, row, col, recv_sem.at[PART, step])
                else:
                    post(src, dst, PART, step, row, col, recv_sem.at[PART, step], home_lo)

        with jax.named_scope("wait_row"):
            for k in (0, 1, 3, 2):
                pieces = vrow[k].at[step, pl.ds(2 - 2 * core, 2)]
                pltpu.make_async_copy(pieces, pieces, mate_sem.at[step, k]).wait()
        with jax.named_scope("mm_row"):
            for y in range(0, Q, 1):
                for n in range(2 * y, 2 * y + 2):
                    total = jnp.zeros((V, 2 * B), jnp.float32)
                    for k in range(Q):
                        hi = lax.rem(c_hi + k, Q)
                        v = jnp.concatenate([vrow[k][step, u] for u in (0, 2, 1, 3)], axis=1)
                        total += block(v, pl.ds(pl.multiple_of(hi * Q * B, Q * B), Q * B), pl.ds(n * 2 * B, 2 * B))
                    last(n, total)
                for ready in range(y, y + 1):
                    emit(ready)

    def meet(step):
        with jax.named_scope("wait_part"):
            arrive(part, PART, step)
        for k in range(Q):
            hi = lax.rem(c_hi + 2 + k, Q)
            total = jnp.zeros((V, B), jnp.float32)
            for lo in range(Q):
                total += part[step, lo * Q + hi].astype(jnp.float32)
            sums_send[step, k] = total.astype(jnp.bfloat16)
            row, col, arrival = c_hi * Q + r_lo, hi * Q + c_lo, recv_sem.at[SUMS, step]
            if k != 2:
                push(sums_send.at[step, k], sums.at[step, r_hi], SUMS, step, row, col, arrival)
            else:
                post(sums_send.at[step, k], sums.at[step, r_hi], SUMS, step, row, col, arrival, home_hi)

    def direct(step):
        def block(v, inner, outer):
            return lax.dot_general(v, tile[outer, inner], (((1,), (1,)), ((), ())), preferred_element_type=jnp.float32)

        def last(n, total):
            acc[n] = total
            dsend[step, n] = acc[n, :, pl.ds(pl.multiple_of((1 - core) * B, B), B)].astype(jnp.bfloat16)

        def emit(part_of):
            for n in range(part_of * Q, part_of * Q + Q):
                to_mate(dsend.at[step, n], exch.at[step, n], EXCH, step, exch_sem.at[step, part_of])

        multiply(step, vcol, col_sem, pl.ds(0, Q), range(Q), block, "col", last, emit)
        meet(step)
        for part_of in range(2):
            mine = exch.at[step, pl.ds(part_of * Q, Q)]
            with jax.named_scope("wait_mate"):
                pltpu.make_async_copy(mine, mine, exch_sem.at[step, part_of]).wait()
            for n in range(part_of * Q, part_of * Q + Q):
                own = acc[n, :, pl.ds(pl.multiple_of(core * B, B), B)]
                dsum[step, n] = (own + exch[step, n].astype(jnp.float32)).astype(jnp.bfloat16)

        for i in range(G // 2):
            n = lax.rem(half + Q + i, G // 2)
            src, dst, arrival = dsum.at[step, n], drecv.at[step, half], recv_sem.at[DIRECT, step]
            if i != Q:
                push(src, dst, DIRECT, step, r, 2 * n + core, arrival)
            else:
                post(src, dst, DIRECT, step, r, 2 * n + core, arrival, True)

    def collect(step):
        applied = jnp.zeros((V, B), jnp.float32)
        with jax.named_scope("wait_drecv"):
            arrive(drecv, DIRECT, step)
        for k in range(G // 2):
            applied += drecv[step, k].astype(jnp.float32)
        with jax.named_scope("wait_sums"):
            arrive(sums, SUMS, step)
        for k in range(Q):
            applied += sums[step, k].astype(jnp.float32)
        now = cur[...]
        mapped = scale_ref[...] * applied - center_shift * now
        factor = jnp.where(step == 0, 1.0 / half_width, 2.0 / half_width)
        updated = factor * mapped - prev[...]
        prev[...] = now
        cur[...] = updated

    def one_step(step, _):
        share(step)

        @pl.when(step == 0)
        def _():
            with jax.named_scope("build"):
                loads[4].wait()
                to_scalars.wait()
                lax.fori_loop(0, G, build, 0)

        with jax.named_scope("hand_over"):
            hand_over(step)
        with jax.named_scope("relay"):
            relay(step)
        transposed(step)
        direct(step)
        collect(step)
        return 0

    lax.fori_loop(0, STEPS, one_step, 0)
    out_ref[...] = cur[...]

    def drain(step, _):
        def sent(kind, buf, n):
            done = buf.at[step, pl.ds(0, n)]
            pltpu.make_async_copy(done, done, send_sem.at[kind, step]).wait()

        for kind, n in ((VROW, G // 2 - 1), (DIRECT, G // 2 - 1), (ROWX, G // 2), (EXCH, G // 2)):
            sent(kind, part, n)
        sent(HOP, hop, Q)
        for kind, buf, n, home, own in ((SUMS, sums, Q, home_hi, 1), (VCOL, part, G, origin_lo == c_lo, Q),
                                        (PART, part, G, home_lo, Q)):
            sent(kind, buf, n - own)

            @pl.when(jnp.logical_not(home))
            def _():
                sent(kind, buf, own)

        return 0

    with jax.named_scope("drain"):
        lax.fori_loop(0, STEPS, drain, 0)


def per_device(start_vectors, scaling, block_values, block_places, block_counts):
    anywhere = pl.BlockSpec(memory_space=pl.ANY)

    def slab(n):
        return pltpu.VMEM((STEPS, n, V, B), jnp.bfloat16)

    f32 = pltpu.VMEM((V, B), jnp.float32)
    return pl.pallas_call(
        kernel,
        name="filter",
        out_shape=jax.ShapeDtypeStruct((V, B), jnp.float32),
        in_specs=[anywhere] * 5,
        out_specs=pl.BlockSpec(memory_space=pltpu.VMEM),
        scratch_shapes=[
            pltpu.VMEM((S + 1, B, B), jnp.bfloat16),
            pltpu.VMEM((G * B, G * B), jnp.bfloat16),
            f32,
            f32,
            pltpu.VMEM((1, B), jnp.float32),
            pltpu.VMEM((2, S), jnp.int32),
            pltpu.VMEM((1, 1), jnp.int32),
            pltpu.VMEM((2, S), jnp.int32),
            pltpu.SMEM((2, S), jnp.int32),
            pltpu.VMEM((STEPS, V, B), jnp.bfloat16),
            slab(Q), *[slab(Q)] * 8, slab(G), slab(G // 2), slab(G), slab(Q), slab(Q), slab(G // 2),
            pltpu.SemaphoreType.DMA((6,)),
            pltpu.SemaphoreType.DMA((8, STEPS)),
            pltpu.SemaphoreType.DMA((8, STEPS)),
            pltpu.SemaphoreType.DMA((STEPS, Q)),
            pltpu.SemaphoreType.DMA((STEPS, Q)),
            pltpu.SemaphoreType.DMA((STEPS, Q)),
            pltpu.SemaphoreType.DMA((STEPS, Q)),
            pltpu.SemaphoreType.DMA((STEPS, 2)),
            pltpu.VMEM((G // 2, V, 2 * B), jnp.float32),
            slab(G // 2), slab(G // 2),
        ],
        compiler_params=pltpu.CompilerParams(collective_id=0, has_side_effects=True, vmem_limit_bytes=60 << 20),
    )(start_vectors, scaling.reshape(1, B), block_places.reshape(2, S), block_counts, block_values.reshape(S, B, B))


def solution(mesh):
    in_specs = (
        P(None, ("row", "col")),
        P(("row", "col")),
        P("row", "col", None, None, None),
        P("row", "col", None, None),
        P("row", "col"),
    )
    out_specs = P(None, ("row", "col"))
    return jax.shard_map(
        per_device, mesh=mesh, in_specs=in_specs, out_specs=out_specs, check_vma=False
    )
```

```python
import jax
import jax.numpy as jnp
from jax import lax
from jax.experimental import pallas as pl
from jax.experimental.pallas import tpu as pltpu
from jax.sharding import PartitionSpec as P

STEPS = 3
G = 16
Q = 4
B = 128
V = 64
S = 128
MESH = pl.DeviceIdType.MESH
VROW, HOP, VCOL, PART, SUMS, DIRECT, ROWX, EXCH = range(8)

center_shift = 0.5
half_width = 3.0


def kernel(x_hbm, scale_hbm, places_hbm, count_hbm, blocks_hbm, out_ref, blk, tile, cur, prev, scale_ref, places, count,
           table_v, table, piece, hop, row0, row1, row2, row3, col0, col1, col2, col3, tsend, dsend, part, sums_send, sums, drecv, in_sem, send_sem, recv_sem,
           hop_sem, row_sem, col_sem, mate_sem, exch_sem, acc, exch, dsum):
    vrow, vcol = (row0, row1, row2, row3), (col0, col1, col2, col3)
    r = lax.axis_index("row")
    c = lax.axis_index("col")
    r_hi, r_lo = r // Q, lax.rem(r, Q)
    c_hi, c_lo = c // Q, lax.rem(c, Q)
    home_hi, home_lo = r_hi == c_hi, r_lo == c_lo
    half, core = c // 2, lax.rem(c, 2)
    mate = c + 1 - 2 * core
    relay_lo = lax.rem(r_lo + Q - 1 + 2 * core, Q)
    origin_lo = lax.rem(r_lo + Q + 1 - 2 * core, Q)

    loads = [
        pltpu.make_async_copy(src, dst, in_sem.at[i])
        for i, (src, dst) in enumerate(((x_hbm, cur), (scale_hbm, scale_ref), (places_hbm, places), (count_hbm, count),
                                        (blocks_hbm, blk.at[pl.ds(0, S)])))
    ]
    for load in loads:
        load.start()

    barrier = pltpu.get_barrier_semaphore()

    def signal(row, col):
        pl.semaphore_signal(barrier, inc=1, device_id=(row, col), device_id_type=MESH)

    for k in range(1, Q):
        signal(lax.rem(r_hi + k, Q) * Q + relay_lo, r_hi * Q + c_lo)
        signal(c_hi * Q + origin_lo, lax.rem(c_hi + k, Q) * Q + c_lo)
        signal(lax.rem(r_hi + k, Q) * Q + r_lo, r_hi * Q + c_lo)

    @pl.when(jnp.logical_not(home_hi))
    def _():
        signal(r_hi * Q + relay_lo, r_hi * Q + c_lo)
        signal(c_hi * Q + origin_lo, c_hi * Q + c_lo)
        for k in range(1, Q):
            signal(c_hi * Q + r_lo, lax.rem(r_hi + k, Q) * Q + c_lo)

    def greet_row(k, _):
        signal(r, lax.rem(c + k, G))
        return 0

    lax.fori_loop(1, G, greet_row, 0)

    def greet_near(k, _):
        signal(r_hi * Q + lax.rem(r_lo + 1 + k // Q, Q), c_hi * Q + lax.rem(k, Q))
        return 0

    lax.fori_loop(0, Q * (Q - 1), greet_near, 0)
    prev[...] = jnp.zeros((V, B), jnp.float32)
    blk[S] = jnp.zeros((B, B), jnp.bfloat16)

    loads[2].wait()
    loads[3].wait()
    lane = lax.broadcasted_iota(jnp.int32, (1, S), 1)
    at = jnp.where(lane < count[...], places[0:1, :] * G + places[1:2, :], -1)
    row_id = lax.broadcasted_iota(jnp.int32, (S, S), 0)
    col_id = lax.broadcasted_iota(jnp.int32, (S, S), 1)
    for upper in range(2):
        slot = jnp.min(jnp.where(row_id + upper * S == at, col_id, S), axis=1, keepdims=True)
        table_v[upper : upper + 1, :] = jnp.min(jnp.where(row_id == col_id, slot, S), axis=0, keepdims=True)
    to_scalars = pltpu.make_async_copy(table_v, table, in_sem.at[5])
    to_scalars.start()
    loads[0].wait()
    loads[1].wait()
    def build(i, _):
        for j in range(G):
            slot = jnp.clip(table[i // 8, lax.rem(i, 8) * G + j], 0, S)
            tile[pl.ds(pl.multiple_of(i * B, B), B), pl.ds(j * B, B)] = blk[slot]
        return 0

    with jax.named_scope("barrier"):
        pl.semaphore_wait(barrier, G - 1 + Q * (Q - 1) + jnp.where(home_hi, 9, 14))

    def push(src, dst, kind, step, row, col, arrival):
        pltpu.make_async_remote_copy(src, dst, send_sem.at[kind, step], arrival, device_id=(row, col), device_id_type=MESH).start()

    def post(src, dst, kind, step, row, col, arrival, own):
        if own is True:
            pltpu.make_async_copy(src, dst, arrival).start()
            return

        @pl.when(own)
        def _():
            pltpu.make_async_copy(src, dst, arrival).start()

        @pl.when(jnp.logical_not(own))
        def _():
            push(src, dst, kind, step, row, col, arrival)

    def to_mate(src, dst, kind, step, arrival):
        pltpu.make_async_remote_copy(src, dst, send_sem.at[kind, step], arrival, device_id=(r, mate),
                                     device_id_type=MESH).start()

    def arrive(buf, kind, step):
        pltpu.make_async_copy(buf.at[step], buf.at[step], recv_sem.at[kind, step]).wait()

    def share(step):
        piece[step] = (scale_ref[...] * cur[...]).astype(jnp.bfloat16)

        for k in (2, 1, 3, 0):
            row, col = lax.rem(r_hi + k, Q) * Q + relay_lo, r_hi * Q + c_lo
            push(piece.at[step], hop.at[step, c_hi], HOP, step, row, col, hop_sem.at[step, c_hi])
        for k in (2, 1, 3, 0):
            hi = lax.rem(c_hi + k, Q)

            for i in range(2):
                there, arrival = vrow[(Q - k) % Q].at[step, 2 * core + c_lo // 2], row_sem.at[step, (Q - k) % Q]
                col = hi * Q + 2 * lax.rem(c_lo // 2 + 1 - i, 2) + core
                if k or not i:
                    push(piece.at[step], there, VROW, step, r, col, arrival)
                else:
                    post(piece.at[step], there, VROW, step, r, col, arrival, True)

    def hand_over(step):
        for k in (0, 1, 3, 2):
            pair = vrow[k].at[step, pl.ds(2 * core, 2)]
            pltpu.make_async_copy(pair, pair, row_sem.at[step, k]).wait()
            for i in range(2):
                both = vrow[k].at[step, 2 * core + i]
                to_mate(both, both, ROWX, step, mate_sem.at[step, k])

    def relay(step):
        for k in (0, 1, 3, 2):
            hi = lax.rem(c_hi + k, Q)
            pltpu.make_async_copy(hop.at[step, hi], hop.at[step, hi], hop_sem.at[step, hi]).wait()

            for i in (2, 1, 3, 0):
                row, col = r_hi * Q + lax.rem(r_lo + i, Q), c_hi * Q + origin_lo
                if i:
                    push(hop.at[step, hi], vcol[k].at[step, c_lo], VCOL, step, row, col, col_sem.at[step, k])
                else:
                    post(hop.at[step, hi], vcol[k].at[step, c_lo], VCOL, step, row, col, col_sem.at[step, k], origin_lo == c_lo)

    def multiply(step, buf, sem, awaited, order, block, name, last, emit):
        for at, k in enumerate((0, 1, 3, 2)):
            hi = lax.rem(c_hi + k, Q)
            pieces = buf[k].at[step, awaited]
            with jax.named_scope("wait_" + name):
                pltpu.make_async_copy(pieces, pieces, sem.at[step, k]).wait()

            def term(n):
                v = jnp.concatenate([buf[k][step, u] for u in order], axis=1)
                total = block(v, pl.ds(pl.multiple_of(hi * Q * B, Q * B), Q * B), pl.ds(n * 2 * B, 2 * B))
                if at:
                    total += acc[n]
                if at < Q - 1:
                    acc[n] = total
                else:
                    last(n, total)

            with jax.named_scope("mm_" + name):
                for part_of in range(2):
                    for n in range(part_of * Q, part_of * Q + Q):
                        term(n)
                    if at == Q - 1:
                        emit(part_of)

    def transposed(step):
        def block(v, inner, outer):
            return jnp.dot(v, tile[inner, outer], preferred_element_type=jnp.float32)

        def last(n, total):
            for u in range(2):
                tsend[step, 2 * n + u] = total[:, u * B : (u + 1) * B].astype(jnp.bfloat16)

        def emit(y):
            for i in range(Q):
                lo = lax.rem(c_lo + i, Q)
                src, dst = tsend.at[step, y * Q + lo], part.at[step, r_lo * Q + y]
                row, col = r_hi * Q + c_lo, c_hi * Q + lo
                if i:
                    push(src, dst, PART, step, row, col, recv_sem.at[PART, step])
                else:
                    post(src, dst, PART, step, row, col, recv_sem.at[PART, step], home_lo)

        with jax.named_scope("wait_row"):
            for k in (0, 1, 3, 2):
                pieces = vrow[k].at[step, pl.ds(2 - 2 * core, 2)]
                pltpu.make_async_copy(pieces, pieces, mate_sem.at[step, k]).wait()
        with jax.named_scope("mm_row"):
            for y in range(0, Q, 1):
                for n in range(2 * y, 2 * y + 2):
                    total = jnp.zeros((V, 2 * B), jnp.float32)
                    for k in range(Q):
                        hi = lax.rem(c_hi + k, Q)
                        v = jnp.concatenate([vrow[k][step, u] for u in (0, 2, 1, 3)], axis=1)
                        total += block(v, pl.ds(pl.multiple_of(hi * Q * B, Q * B), Q * B), pl.ds(n * 2 * B, 2 * B))
                    last(n, total)
                for ready in range(y, y + 1):
                    emit(ready)

    def meet(step):
        with jax.named_scope("wait_part"):
            arrive(part, PART, step)
        for k in range(Q):
            hi = lax.rem(c_hi + 2 + k, Q)
            total = jnp.zeros((V, B), jnp.float32)
            for lo in range(Q):
                total += part[step, lo * Q + hi].astype(jnp.float32)
            sums_send[step, k] = total.astype(jnp.bfloat16)
            row, col, arrival = c_hi * Q + r_lo, hi * Q + c_lo, recv_sem.at[SUMS, step]
            if k != 2:
                push(sums_send.at[step, k], sums.at[step, r_hi], SUMS, step, row, col, arrival)
            else:
                post(sums_send.at[step, k], sums.at[step, r_hi], SUMS, step, row, col, arrival, home_hi)

    def direct(step):
        def block(v, inner, outer):
            return lax.dot_general(v, tile[outer, inner], (((1,), (1,)), ((), ())), preferred_element_type=jnp.float32)

        def last(n, total):
            acc[n] = total
            dsend[step, n] = acc[n, :, pl.ds(pl.multiple_of((1 - core) * B, B), B)].astype(jnp.bfloat16)

        def emit(part_of):
            for n in range(part_of * Q, part_of * Q + Q):
                to_mate(dsend.at[step, n], exch.at[step, n], EXCH, step, exch_sem.at[step, part_of])

        multiply(step, vcol, col_sem, pl.ds(0, Q), range(Q), block, "col", last, emit)
        meet(step)
        for part_of in range(2):
            mine = exch.at[step, pl.ds(part_of * Q, Q)]
            with jax.named_scope("wait_mate"):
                pltpu.make_async_copy(mine, mine, exch_sem.at[step, part_of]).wait()
            for n in range(part_of * Q, part_of * Q + Q):
                own = acc[n, :, pl.ds(pl.multiple_of(core * B, B), B)]
                dsum[step, n] = (own + exch[step, n].astype(jnp.float32)).astype(jnp.bfloat16)
            for n in range(part_of * Q, part_of * Q + Q):
                post(dsum.at[step, n], drecv.at[step, half], DIRECT, step, r, 2 * n + core, recv_sem.at[DIRECT, step], half == n)

    def collect(step):
        applied = jnp.zeros((V, B), jnp.float32)
        with jax.named_scope("wait_drecv"):
            arrive(drecv, DIRECT, step)
        for k in range(G // 2):
            applied += drecv[step, k].astype(jnp.float32)
        with jax.named_scope("wait_sums"):
            arrive(sums, SUMS, step)
        for k in range(Q):
            applied += sums[step, k].astype(jnp.float32)
        now = cur[...]
        mapped = scale_ref[...] * applied - center_shift * now
        factor = jnp.where(step == 0, 1.0 / half_width, 2.0 / half_width)
        updated = factor * mapped - prev[...]
        prev[...] = now
        cur[...] = updated

    def one_step(step, _):
        share(step)

        @pl.when(step == 0)
        def _():
            with jax.named_scope("build"):
                loads[4].wait()
                to_scalars.wait()
                lax.fori_loop(0, G, build, 0)

        with jax.named_scope("hand_over"):
            hand_over(step)
        with jax.named_scope("relay"):
            relay(step)
        transposed(step)
        direct(step)
        collect(step)
        return 0

    lax.fori_loop(0, STEPS, one_step, 0)
    out_ref[...] = cur[...]

    def drain(step, _):
        def sent(kind, buf, n):
            done = buf.at[step, pl.ds(0, n)]
            pltpu.make_async_copy(done, done, send_sem.at[kind, step]).wait()

        for kind, n in ((VROW, G // 2 - 1), (DIRECT, G // 2 - 1), (ROWX, G // 2), (EXCH, G // 2)):
            sent(kind, part, n)
        sent(HOP, hop, Q)
        for kind, buf, n, home, own in ((SUMS, sums, Q, home_hi, 1), (VCOL, part, G, origin_lo == c_lo, Q),
                                        (PART, part, G, home_lo, Q)):
            sent(kind, buf, n - own)

            @pl.when(jnp.logical_not(home))
            def _():
                sent(kind, buf, own)

        return 0

    with jax.named_scope("drain"):
        lax.fori_loop(0, STEPS, drain, 0)


def per_device(start_vectors, scaling, block_values, block_places, block_counts):
    anywhere = pl.BlockSpec(memory_space=pl.ANY)

    def slab(n):
        return pltpu.VMEM((STEPS, n, V, B), jnp.bfloat16)

    f32 = pltpu.VMEM((V, B), jnp.float32)
    return pl.pallas_call(
        kernel,
        name="filter",
        out_shape=jax.ShapeDtypeStruct((V, B), jnp.float32),
        in_specs=[anywhere] * 5,
        out_specs=pl.BlockSpec(memory_space=pltpu.VMEM),
        scratch_shapes=[
            pltpu.VMEM((S + 1, B, B), jnp.bfloat16),
            pltpu.VMEM((G * B, G * B), jnp.bfloat16),
            f32,
            f32,
            pltpu.VMEM((1, B), jnp.float32),
            pltpu.VMEM((2, S), jnp.int32),
            pltpu.VMEM((1, 1), jnp.int32),
            pltpu.VMEM((2, S), jnp.int32),
            pltpu.SMEM((2, S), jnp.int32),
            pltpu.VMEM((STEPS, V, B), jnp.bfloat16),
            slab(Q), *[slab(Q)] * 8, slab(G), slab(G // 2), slab(G), slab(Q), slab(Q), slab(G // 2),
            pltpu.SemaphoreType.DMA((6,)),
            pltpu.SemaphoreType.DMA((8, STEPS)),
            pltpu.SemaphoreType.DMA((8, STEPS)),
            pltpu.SemaphoreType.DMA((STEPS, Q)),
            pltpu.SemaphoreType.DMA((STEPS, Q)),
            pltpu.SemaphoreType.DMA((STEPS, Q)),
            pltpu.SemaphoreType.DMA((STEPS, Q)),
            pltpu.SemaphoreType.DMA((STEPS, 2)),
            pltpu.VMEM((G // 2, V, 2 * B), jnp.float32),
            slab(G // 2), slab(G // 2),
        ],
        compiler_params=pltpu.CompilerParams(collective_id=0, has_side_effects=True, vmem_limit_bytes=60 << 20),
    )(start_vectors, scaling.reshape(1, B), block_places.reshape(2, S), block_counts, block_values.reshape(S, B, B))


def solution(mesh):
    in_specs = (
        P(None, ("row", "col")),
        P(("row", "col")),
        P("row", "col", None, None, None),
        P("row", "col", None, None),
        P("row", "col"),
    )
    out_specs = P(None, ("row", "col"))
    return jax.shard_map(
        per_device, mesh=mesh, in_specs=in_specs, out_specs=out_specs, check_vma=False
    )
```

```python
import jax
import jax.numpy as jnp
from jax import lax
from jax.experimental import pallas as pl
from jax.experimental.pallas import tpu as pltpu
from jax.sharding import PartitionSpec as P

STEPS = 3
G = 16
Q = 4
B = 128
V = 64
S = 128
MESH = pl.DeviceIdType.MESH
VROW, HOP, VCOL, PART, SUMS, DIRECT, ROWX, EXCH = range(8)

center_shift = 0.5
half_width = 3.0


def kernel(x_hbm, scale_hbm, places_hbm, count_hbm, blocks_hbm, out_ref, blk, tile, cur, prev, scale_ref, places, count,
           table_v, table, piece, hop, row0, row1, row2, row3, col0, col1, col2, col3, tsend, dsend, part, sums_send, sums, drecv, in_sem, send_sem, recv_sem,
           hop_sem, row_sem, col_sem, mate_sem, exch_sem, acc, exch, dsum):
    vrow, vcol = (row0, row1, row2, row3), (col0, col1, col2, col3)
    r = lax.axis_index("row")
    c = lax.axis_index("col")
    r_hi, r_lo = r // Q, lax.rem(r, Q)
    c_hi, c_lo = c // Q, lax.rem(c, Q)
    home_hi, home_lo = r_hi == c_hi, r_lo == c_lo
    half, core = c // 2, lax.rem(c, 2)
    mate = c + 1 - 2 * core
    relay_lo = lax.rem(r_lo + Q - 1 + 2 * core, Q)
    origin_lo = lax.rem(r_lo + Q + 1 - 2 * core, Q)

    loads = [
        pltpu.make_async_copy(src, dst, in_sem.at[i])
        for i, (src, dst) in enumerate(((x_hbm, cur), (scale_hbm, scale_ref), (places_hbm, places), (count_hbm, count),
                                        (blocks_hbm, blk.at[pl.ds(0, S)])))
    ]
    for load in loads:
        load.start()

    barrier = pltpu.get_barrier_semaphore()

    def signal(row, col):
        pl.semaphore_signal(barrier, inc=1, device_id=(row, col), device_id_type=MESH)

    for k in range(1, Q):
        signal(lax.rem(r_hi + k, Q) * Q + relay_lo, r_hi * Q + c_lo)
        signal(c_hi * Q + origin_lo, lax.rem(c_hi + k, Q) * Q + c_lo)
        signal(lax.rem(r_hi + k, Q) * Q + r_lo, r_hi * Q + c_lo)

    @pl.when(jnp.logical_not(home_hi))
    def _():
        signal(r_hi * Q + relay_lo, r_hi * Q + c_lo)
        signal(c_hi * Q + origin_lo, c_hi * Q + c_lo)
        for k in range(1, Q):
            signal(c_hi * Q + r_lo, lax.rem(r_hi + k, Q) * Q + c_lo)

    def greet_row(k, _):
        signal(r, lax.rem(c + k, G))
        return 0

    lax.fori_loop(1, G, greet_row, 0)

    def greet_near(k, _):
        signal(r_hi * Q + lax.rem(r_lo + 1 + k // Q, Q), c_hi * Q + lax.rem(k, Q))
        return 0

    lax.fori_loop(0, Q * (Q - 1), greet_near, 0)
    prev[...] = jnp.zeros((V, B), jnp.float32)
    blk[S] = jnp.zeros((B, B), jnp.bfloat16)

    loads[2].wait()
    loads[3].wait()
    lane = lax.broadcasted_iota(jnp.int32, (1, S), 1)
    at = jnp.where(lane < count[...], places[0:1, :] * G + places[1:2, :], -1)
    row_id = lax.broadcasted_iota(jnp.int32, (S, S), 0)
    col_id = lax.broadcasted_iota(jnp.int32, (S, S), 1)
    for upper in range(2):
        slot = jnp.min(jnp.where(row_id + upper * S == at, col_id, S), axis=1, keepdims=True)
        table_v[upper : upper + 1, :] = jnp.min(jnp.where(row_id == col_id, slot, S), axis=0, keepdims=True)
    to_scalars = pltpu.make_async_copy(table_v, table, in_sem.at[5])
    to_scalars.start()
    loads[0].wait()
    loads[1].wait()
    def build(i, _):
        for j in range(G):
            slot = jnp.clip(table[i // 8, lax.rem(i, 8) * G + j], 0, S)
            tile[pl.ds(pl.multiple_of(i * B, B), B), pl.ds(j * B, B)] = blk[slot]
        return 0

    with jax.named_scope("barrier"):
        pl.semaphore_wait(barrier, G - 1 + Q * (Q - 1) + jnp.where(home_hi, 9, 14))

    def push(src, dst, kind, step, row, col, arrival):
        pltpu.make_async_remote_copy(src, dst, send_sem.at[kind, step], arrival, device_id=(row, col), device_id_type=MESH).start()

    def post(src, dst, kind, step, row, col, arrival, own):
        if own is True:
            pltpu.make_async_copy(src, dst, arrival).start()
            return

        @pl.when(own)
        def _():
            pltpu.make_async_copy(src, dst, arrival).start()

        @pl.when(jnp.logical_not(own))
        def _():
            push(src, dst, kind, step, row, col, arrival)

    def to_mate(src, dst, kind, step, arrival):
        pltpu.make_async_remote_copy(src, dst, send_sem.at[kind, step], arrival, device_id=(r, mate),
                                     device_id_type=MESH).start()

    def arrive(buf, kind, step):
        pltpu.make_async_copy(buf.at[step], buf.at[step], recv_sem.at[kind, step]).wait()

    def share(step):
        piece[step] = (scale_ref[...] * cur[...]).astype(jnp.bfloat16)

        for k in (2, 1, 3, 0):
            row, col = lax.rem(r_hi + k, Q) * Q + relay_lo, r_hi * Q + c_lo
            push(piece.at[step], hop.at[step, c_hi], HOP, step, row, col, hop_sem.at[step, c_hi])
        for k in (2, 1, 3, 0):
            hi = lax.rem(c_hi + k, Q)

            for i in range(2):
                there, arrival = vrow[(Q - k) % Q].at[step, 2 * core + c_lo // 2], row_sem.at[step, (Q - k) % Q]
                col = hi * Q + 2 * lax.rem(c_lo // 2 + 1 - i, 2) + core
                if k or not i:
                    push(piece.at[step], there, VROW, step, r, col, arrival)
                else:
                    post(piece.at[step], there, VROW, step, r, col, arrival, True)

    def hand_over(step):
        for k in (0, 1, 3, 2):
            pair = vrow[k].at[step, pl.ds(2 * core, 2)]
            pltpu.make_async_copy(pair, pair, row_sem.at[step, k]).wait()
            for i in range(2):
                both = vrow[k].at[step, 2 * core + i]
                to_mate(both, both, ROWX, step, mate_sem.at[step, k])

    def relay(step):
        for k in (0, 1, 3, 2):
            hi = lax.rem(c_hi + k, Q)
            pltpu.make_async_copy(hop.at[step, hi], hop.at[step, hi], hop_sem.at[step, hi]).wait()

            for i in (2, 1, 3, 0):
                row, col = r_hi * Q + lax.rem(r_lo + i, Q), c_hi * Q + origin_lo
                if i:
                    push(hop.at[step, hi], vcol[k].at[step, c_lo], VCOL, step, row, col, col_sem.at[step, k])
                else:
                    post(hop.at[step, hi], vcol[k].at[step, c_lo], VCOL, step, row, col, col_sem.at[step, k], origin_lo == c_lo)

    def multiply(step, buf, sem, awaited, order, block, name, last, emit):
        for at, k in enumerate((0, 1, 3, 2)):
            hi = lax.rem(c_hi + k, Q)
            pieces = buf[k].at[step, awaited]
            with jax.named_scope("wait_" + name):
                pltpu.make_async_copy(pieces, pieces, sem.at[step, k]).wait()

            def term(n):
                v = jnp.concatenate([buf[k][step, u] for u in order], axis=1)
                total = block(v, pl.ds(pl.multiple_of(hi * Q * B, Q * B), Q * B), pl.ds(n * 2 * B, 2 * B))
                if at:
                    total += acc[n]
                if at < Q - 1:
                    acc[n] = total
                else:
                    last(n, total)

            with jax.named_scope("mm_" + name):
                for part_of in range(Q):
                    for n in range(part_of * 2, part_of * 2 + 2):
                        term(n)
                    if at == Q - 1:
                        emit(part_of)

    def transposed(step):
        def block(v, inner, outer):
            return jnp.dot(v, tile[inner, outer], preferred_element_type=jnp.float32)

        def last(n, total):
            for u in range(2):
                tsend[step, 2 * n + u] = total[:, u * B : (u + 1) * B].astype(jnp.bfloat16)

        def emit(y):
            for i in range(Q):
                lo = lax.rem(c_lo + i, Q)
                src, dst = tsend.at[step, y * Q + lo], part.at[step, r_lo * Q + y]
                row, col = r_hi * Q + c_lo, c_hi * Q + lo
                if i:
                    push(src, dst, PART, step, row, col, recv_sem.at[PART, step])
                else:
                    post(src, dst, PART, step, row, col, recv_sem.at[PART, step], home_lo)

        with jax.named_scope("wait_row"):
            for k in (0, 1, 3, 2):
                pieces = vrow[k].at[step, pl.ds(2 - 2 * core, 2)]
                pltpu.make_async_copy(pieces, pieces, mate_sem.at[step, k]).wait()
        with jax.named_scope("mm_row"):
            for y in range(0, Q, 1):
                for n in range(2 * y, 2 * y + 2):
                    total = jnp.zeros((V, 2 * B), jnp.float32)
                    for k in range(Q):
                        hi = lax.rem(c_hi + k, Q)
                        v = jnp.concatenate([vrow[k][step, u] for u in (0, 2, 1, 3)], axis=1)
                        total += block(v, pl.ds(pl.multiple_of(hi * Q * B, Q * B), Q * B), pl.ds(n * 2 * B, 2 * B))
                    last(n, total)
                for ready in range(y, y + 1):
                    emit(ready)

    def meet(step):
        with jax.named_scope("wait_part"):
            arrive(part, PART, step)
        for k in range(Q):
            hi = lax.rem(c_hi + 2 + k, Q)
            total = jnp.zeros((V, B), jnp.float32)
            for lo in range(Q):
                total += part[step, lo * Q + hi].astype(jnp.float32)
            sums_send[step, k] = total.astype(jnp.bfloat16)
            row, col, arrival = c_hi * Q + r_lo, hi * Q + c_lo, recv_sem.at[SUMS, step]
            if k != 2:
                push(sums_send.at[step, k], sums.at[step, r_hi], SUMS, step, row, col, arrival)
            else:
                post(sums_send.at[step, k], sums.at[step, r_hi], SUMS, step, row, col, arrival, home_hi)

    def direct(step):
        def block(v, inner, outer):
            return lax.dot_general(v, tile[outer, inner], (((1,), (1,)), ((), ())), preferred_element_type=jnp.float32)

        def last(n, total):
            acc[n] = total
            dsend[step, n] = acc[n, :, pl.ds(pl.multiple_of((1 - core) * B, B), B)].astype(jnp.bfloat16)

        def emit(part_of):
            for n in range(part_of * 2, part_of * 2 + 2):
                to_mate(dsend.at[step, n], exch.at[step, n], EXCH, step, exch_sem.at[step, part_of])

        multiply(step, vcol, col_sem, pl.ds(0, Q), range(Q), block, "col", last, emit)
        meet(step)
        for part_of in range(Q):
            mine = exch.at[step, pl.ds(part_of * 2, 2)]
            with jax.named_scope("wait_mate"):
                pltpu.make_async_copy(mine, mine, exch_sem.at[step, part_of]).wait()
            for n in range(part_of * 2, part_of * 2 + 2):
                own = acc[n, :, pl.ds(pl.multiple_of(core * B, B), B)]
                dsum[step, n] = (own + exch[step, n].astype(jnp.float32)).astype(jnp.bfloat16)
            for n in range(part_of * 2, part_of * 2 + 2):
                post(dsum.at[step, n], drecv.at[step, half], DIRECT, step, r, 2 * n + core, recv_sem.at[DIRECT, step], half == n)

    def collect(step):
        applied = jnp.zeros((V, B), jnp.float32)
        with jax.named_scope("wait_drecv"):
            arrive(drecv, DIRECT, step)
        for k in range(G // 2):
            applied += drecv[step, k].astype(jnp.float32)
        with jax.named_scope("wait_sums"):
            arrive(sums, SUMS, step)
        for k in range(Q):
            applied += sums[step, k].astype(jnp.float32)
        now = cur[...]
        mapped = scale_ref[...] * applied - center_shift * now
        factor = jnp.where(step == 0, 1.0 / half_width, 2.0 / half_width)
        updated = factor * mapped - prev[...]
        prev[...] = now
        cur[...] = updated

    def one_step(step, _):
        share(step)

        @pl.when(step == 0)
        def _():
            with jax.named_scope("build"):
                loads[4].wait()
                to_scalars.wait()
                lax.fori_loop(0, G, build, 0)

        with jax.named_scope("hand_over"):
            hand_over(step)
        with jax.named_scope("relay"):
            relay(step)
        transposed(step)
        direct(step)
        collect(step)
        return 0

    lax.fori_loop(0, STEPS, one_step, 0)
    out_ref[...] = cur[...]

    def drain(step, _):
        def sent(kind, buf, n):
            done = buf.at[step, pl.ds(0, n)]
            pltpu.make_async_copy(done, done, send_sem.at[kind, step]).wait()

        for kind, n in ((VROW, G // 2 - 1), (DIRECT, G // 2 - 1), (ROWX, G // 2), (EXCH, G // 2)):
            sent(kind, part, n)
        sent(HOP, hop, Q)
        for kind, buf, n, home, own in ((SUMS, sums, Q, home_hi, 1), (VCOL, part, G, origin_lo == c_lo, Q),
                                        (PART, part, G, home_lo, Q)):
            sent(kind, buf, n - own)

            @pl.when(jnp.logical_not(home))
            def _():
                sent(kind, buf, own)

        return 0

    with jax.named_scope("drain"):
        lax.fori_loop(0, STEPS, drain, 0)


def per_device(start_vectors, scaling, block_values, block_places, block_counts):
    anywhere = pl.BlockSpec(memory_space=pl.ANY)

    def slab(n):
        return pltpu.VMEM((STEPS, n, V, B), jnp.bfloat16)

    f32 = pltpu.VMEM((V, B), jnp.float32)
    return pl.pallas_call(
        kernel,
        name="filter",
        out_shape=jax.ShapeDtypeStruct((V, B), jnp.float32),
        in_specs=[anywhere] * 5,
        out_specs=pl.BlockSpec(memory_space=pltpu.VMEM),
        scratch_shapes=[
            pltpu.VMEM((S + 1, B, B), jnp.bfloat16),
            pltpu.VMEM((G * B, G * B), jnp.bfloat16),
            f32,
            f32,
            pltpu.VMEM((1, B), jnp.float32),
            pltpu.VMEM((2, S), jnp.int32),
            pltpu.VMEM((1, 1), jnp.int32),
            pltpu.VMEM((2, S), jnp.int32),
            pltpu.SMEM((2, S), jnp.int32),
            pltpu.VMEM((STEPS, V, B), jnp.bfloat16),
            slab(Q), *[slab(Q)] * 8, slab(G), slab(G // 2), slab(G), slab(Q), slab(Q), slab(G // 2),
            pltpu.SemaphoreType.DMA((6,)),
            pltpu.SemaphoreType.DMA((8, STEPS)),
            pltpu.SemaphoreType.DMA((8, STEPS)),
            pltpu.SemaphoreType.DMA((STEPS, Q)),
            pltpu.SemaphoreType.DMA((STEPS, Q)),
            pltpu.SemaphoreType.DMA((STEPS, Q)),
            pltpu.SemaphoreType.DMA((STEPS, Q)),
            pltpu.SemaphoreType.DMA((STEPS, Q)),
            pltpu.VMEM((G // 2, V, 2 * B), jnp.float32),
            slab(G // 2), slab(G // 2),
        ],
        compiler_params=pltpu.CompilerParams(collective_id=0, has_side_effects=True, vmem_limit_bytes=60 << 20),
    )(start_vectors, scaling.reshape(1, B), block_places.reshape(2, S), block_counts, block_values.reshape(S, B, B))


def solution(mesh):
    in_specs = (
        P(None, ("row", "col")),
        P(("row", "col")),
        P("row", "col", None, None, None),
        P("row", "col", None, None),
        P("row", "col"),
    )
    out_specs = P(None, ("row", "col"))
    return jax.shard_map(
        per_device, mesh=mesh, in_specs=in_specs, out_specs=out_specs, check_vma=False
    )
```
